32 devices in a mesh: front: 4 (over y, core), row: 4 (over z), col: 2 (over x).
Axes of the slice: x: 2, y: 2, z: 4, core: 2. Of those that a mesh axis runs over, the one named last changes fastest.
Arguments:
- pivot_block: bfloat16 [4, 1024, 1024], P('front'), may hold values from -6 to 6
- border: bfloat16 [4, 8192, 1024], P('front', 'row'), may hold values from -6 to 6
- contrib: bfloat16 [4, 8192, 8192], P('front', 'row', 'col'), may hold values from -6 to 6
- inverses: bfloat16 [4, 4, 256, 256], P('front'), may hold values from -0.0625 to 0.0625
- row_tiles: int32 [4, 64], replicated, may hold values from 0 to 79, as said below
- col_tiles: int32 [4, 64], replicated, may hold values from 0 to 79, as said below
- owner: int32 [80], replicated, may hold values from 0 to 79, as said below
- schur_init: bfloat16 [10240, 10240], P(('front', 'row'), 'col'), may hold values from -6 to 6
- block: bfloat16 [10240, 512], P('col'), may hold values from -0.0625 to 0.0625
Outputs:
- schur: float32 [10240, 10240], P(('front', 'row'), 'col')
- product: float32 [10240, 512], P(('front', 'row', 'col'))
The draws below stay inside these ranges and needn't reach their ends.
Inputs may be any that keep to these rules, and one draw needn't show every extreme that they name: owner is a permutation of 0 .. 79. For each front the 64 entries are distinct. With s = owner[row_tiles[f, i]], each front has exactly 4 entries in each group s // 5; among the 16 entries of one aligned block of a front at most 2 fall in one group, and that many in some block of every draw. For each front the 64 entries are distinct. With s = owner[col_tiles[f, j]], each front has exactly 32 entries in each group s // 40; among the 32 entries of one aligned block of a front at most 32 fall in one group, and that many in some block of every draw.
All inputs are finite; a program needn't handle non-finite values.
Results may differ from the reference program's by a relative error of at most 0.008.
Values may be sent and summed in bfloat16 or wider, within the bound.
No kernel may reach another device: no remote copies, remote signals or barrier semaphores. Data moves between devices by JAX's collectives and lax.ppermute only.
A program may use at most 256 MiB of HBM per device.

```python
import jax
import jax.numpy as jnp

C = 8192
NB = 256
PANELS = 4
TILE = 128
SN = 10240
BW = 512
FRONTS = 4
P_SIZE = 1024
CT = 64
ST = 80
N_FRONT = 4
N_ROW = 4
N_COL = 2


def tile_layout(key, blocks, groups, per_group, used):
    total = groups * used
    base = total // (blocks * groups)
    flips = jax.random.randint(jax.random.fold_in(key, 1), (blocks // 2, groups // 2), -1, 2)
    flips = flips.at[0, 0].set(1)
    stepped = flips * base
    pattern = jnp.stack([jnp.stack([stepped, -stepped], -1), jnp.stack([-stepped, stepped], -1)], 1)
    counts = base + pattern.reshape(blocks, groups)
    group_keys = jax.random.split(jax.random.fold_in(key, 2), groups)
    chosen = jax.vmap(lambda single: jnp.sort(jax.random.permutation(single, per_group)[:used]))(group_keys)
    running = jnp.cumsum(counts, axis=0)
    holder = jnp.sum((running[:, :, None] <= jnp.arange(used)[None, None, :]).astype(jnp.int32), axis=0)
    shuffle = jax.random.permutation(jax.random.fold_in(key, 3), total)
    scores = holder.reshape(-1) * total + shuffle
    ordering = jnp.argsort(scores)
    slots = (jnp.arange(groups)[:, None] * per_group + chosen).reshape(-1)
    return slots[ordering].astype(jnp.int32)


def draw_owner(key, part):
    return jax.random.permutation(jax.random.fold_in(key, 7), ST).astype(jnp.int32)


def draw_row_tiles(key, part):
    inverse_map = jnp.argsort(draw_owner(key, part)).astype(jnp.int32)
    groups = N_FRONT * N_ROW
    lists = [inverse_map[tile_layout(jax.random.fold_in(key, 100 + front_index), N_ROW, groups, ST // groups, CT // groups)] for front_index in range(FRONTS)]
    return jnp.stack(lists).astype(jnp.int32)


def draw_col_tiles(key, part):
    inverse_map = jnp.argsort(draw_owner(key, part)).astype(jnp.int32)
    lists = [inverse_map[tile_layout(jax.random.fold_in(key, 200 + front_index), N_COL, N_COL, ST // N_COL, CT // N_COL)] for front_index in range(FRONTS)]
    return jnp.stack(lists).astype(jnp.int32)


def block_scale(key, shape, shards, smallest, top_value):
    factor_of, own = 1.0, jax.random.fold_in(key, 6)
    for position, parts in shards:
        draws = jnp.exp(jax.random.uniform(jax.random.fold_in(own, position), (parts,), jnp.float32, smallest / len(shards), top_value / len(shards)))
        factor_of = factor_of * jnp.repeat(draws, shape[position] // parts).reshape([-1 if axis == position else 1 for axis in range(len(shape))])
    return factor_of


def noise(key, dims, scale, most, cuts=(), dtype=jnp.bfloat16):
    level = block_scale(key, dims, cuts, -0.22, 0.18) if cuts else 1.0
    entries = jax.random.normal(key, dims, jnp.float32) * scale * level
    return jnp.minimum(jnp.maximum(entries, -most), most).astype(dtype)


def setup_inputs(seed: int = 0) -> dict:
    seeds = jax.random.split(jax.random.key(seed), 10)
    pivot_block = noise(seeds[0], (FRONTS, P_SIZE, P_SIZE), 1.0, 6.0, ((0, 4),))
    border = noise(seeds[1], (FRONTS, C, P_SIZE), 1.0, 6.0, ((0, 4), (1, 4)))
    contrib = noise(seeds[2], (FRONTS, C, C), 1.0, 6.0, ((0, 4), (1, 4), (2, 2)))
    inverses = noise(seeds[3], (FRONTS, PANELS, NB, NB), (32 * NB) ** -0.5, 0.0625, ((0, 4),))
    row_tiles = draw_row_tiles(jax.random.fold_in(seeds[9], 71), 0)
    col_tiles = draw_col_tiles(jax.random.fold_in(seeds[9], 71), 0)
    owner = draw_owner(jax.random.fold_in(seeds[9], 71), 0)
    schur_init = noise(seeds[7], (SN, SN), 1.0, 6.0, ((0, 16), (1, 2)))
    block = noise(seeds[8], (SN, BW), SN ** -0.5, 0.0625, ((0, 2),))
    return {"pivot_block": pivot_block, "border": border, "contrib": contrib, "inverses": inverses, "row_tiles": row_tiles, "col_tiles": col_tiles, "owner": owner, "schur_init": schur_init, "block": block}


def eliminate(pivot, rows, inverse_set):
    pivot_now = pivot.astype(jnp.float32)
    rows_now = rows.astype(jnp.float32)
    leaves = []
    for panel_index in range(PANELS):
        start = panel_index * NB
        left = pivot_now[:, start:start + NB].astype(jnp.bfloat16)
        below = jnp.arange(P_SIZE)[:, None] >= start + NB
        lower = jnp.where(below, jnp.dot(left, inverse_set[panel_index], preferred_element_type=jnp.float32), 0.0).astype(jnp.bfloat16)
        side = jnp.dot(rows_now[:, start:start + NB].astype(jnp.bfloat16), inverse_set[panel_index], preferred_element_type=jnp.float32).astype(jnp.bfloat16)
        pivot_now = pivot_now - jnp.dot(lower, lower.T, preferred_element_type=jnp.float32)
        rows_now = rows_now - jnp.dot(side, lower.T, preferred_element_type=jnp.float32)
        leaves.append(side)
    return jnp.concatenate(leaves, axis=1)


def reference(pivot_block, border, contrib, inverses, row_tiles, col_tiles, owner, schur_init, block):
    slot_rows = owner[row_tiles]
    slot_cols = owner[col_tiles]
    tiled = jnp.zeros((ST, ST, TILE, TILE), jnp.float32)
    for front_index in range(FRONTS):
        factor = eliminate(pivot_block[front_index], border[front_index], inverses[front_index])
        update = (contrib[front_index].astype(jnp.float32) - jnp.dot(factor, factor.T, preferred_element_type=jnp.float32)).astype(jnp.bfloat16)
        pieces = update.astype(jnp.float32).reshape(CT, TILE, CT, TILE).transpose(0, 2, 1, 3)
        tiled = tiled.at[slot_rows[front_index][:, None], slot_cols[front_index][None, :]].add(pieces)
    schur = schur_init.astype(jnp.float32) + tiled.transpose(0, 2, 1, 3).reshape(SN, SN)
    product = jnp.dot(schur.astype(jnp.bfloat16), block, preferred_element_type=jnp.float32)
    return (schur, product)
```

```python
import jax
import jax.numpy as jnp
from jax import lax
from jax.experimental import pallas as pl
from jax.experimental.pallas import tpu as pltpu
from jax.sharding import PartitionSpec as P

TILE = 128
CHUNKS = 4
ADJACENT = 8
FR = ("front", "row")


def eliminate(pivot, rows, inverse_set):
    panels = inverse_set.shape[0]
    width = inverse_set.shape[1]
    pivot_now = pivot.astype(jnp.float32)
    rows_now = rows.astype(jnp.float32)
    leaves = []
    for panel_index in range(panels):
        start = panel_index * width
        left = pivot_now[:, start : start + width].astype(jnp.bfloat16)
        below = jnp.arange(pivot.shape[0])[:, None] >= start + width
        lower = jnp.where(
            below, jnp.dot(left, inverse_set[panel_index], preferred_element_type=jnp.float32), 0.0
        ).astype(jnp.bfloat16)
        side = jnp.dot(
            rows_now[:, start : start + width].astype(jnp.bfloat16),
            inverse_set[panel_index],
            preferred_element_type=jnp.float32,
        ).astype(jnp.bfloat16)
        pivot_now = pivot_now - lax.dot_general(
            lower, lower, (((1,), (1,)), ((), ())), preferred_element_type=jnp.float32
        )
        rows_now = rows_now - lax.dot_general(
            side, lower, (((1,), (1,)), ((), ())), preferred_element_type=jnp.float32
        )
        leaves.append(side)
    return jnp.concatenate(leaves, axis=1)


def count(mask, axis=-1):
    return jnp.sum(mask.astype(jnp.int32), axis=axis)


def earlier(n):
    return jnp.arange(n)[None, :] < jnp.arange(n)[:, None]


def row_plan(slot_rows, per_group, groups, adjacent):
    sources, tile_rows = slot_rows.shape
    target = slot_rows // per_group
    within = slot_rows % per_group
    same = target[:, :, None] == target[:, None, :]
    rank = count(same & earlier(tile_rows)[None])
    extra = rank > 0
    key = target * tile_rows + rank
    extra_order = count(extra[:, None, :] & (key[:, None, :] < key[:, :, None]))
    empty = count(target[:, None, :] == jnp.arange(groups)[None, :, None]) == 0
    empty_order = count(empty[:, None, :] & earlier(groups)[None])
    lands = jnp.where(
        extra[:, None, :],
        empty[:, :, None] & (empty_order[:, :, None] == extra_order[:, None, :]),
        target[:, None, :] == jnp.arange(groups)[None, :, None],
    ).astype(jnp.int32)
    source_row = jnp.sum(lands * jnp.arange(tile_rows), axis=-1)
    to_group = jnp.sum(lands * target[:, None, :], axis=-1)
    to_within = jnp.sum(lands * within[:, None, :], axis=-1)
    here = jnp.arange(groups)[None, :]
    astray = to_group != here
    order = count(
        (to_group[:, None, :] == to_group[None, :, :])
        & astray[None]
        & earlier(sources)[:, :, None],
        axis=1,
    )
    near = astray & (to_group == (here ^ 1)) & (order < adjacent)
    far = astray & ~near
    far_round = jnp.where(to_group == (here ^ 1), order - adjacent, order)
    rounds = jnp.max(jnp.where(far, far_round + 1, 0))
    flat_group = to_group.T.reshape(-1)
    flat_far = far.T.reshape(-1)
    total = flat_group.shape[0]
    far_place = count(
        (flat_group[None, :] == flat_group[:, None]) & flat_far[None, :] & earlier(total)
    ).reshape(groups, sources).T
    return dict(
        source_row=source_row,
        to_group=to_group,
        to_within=to_within,
        order=order,
        near=near,
        far=far,
        far_round=far_round,
        far_place=far_place,
        astray=astray,
        rounds=rounds,
    )


def unwritten(shape, dtype):
    return pl.pallas_call(
        lambda out: None,
        out_shape=jax.ShapeDtypeStruct(shape, dtype),
        out_specs=pl.BlockSpec(memory_space=pl.ANY),
    )()


def update_kernel(parts, scalars, *refs):
    left = refs[:parts]
    right = refs[parts]
    old = refs[parts + 1 : 2 * parts + 1]
    out = refs[2 * parts + 1]
    lhs = jnp.concatenate([part[0] for part in left], axis=0)
    change = lax.dot_general(
        lhs, right[...], (((1,), (1,)), ((), ())), preferred_element_type=jnp.float32
    )
    for part in range(parts):
        new = old[part][...].astype(jnp.float32) - change[part * TILE : (part + 1) * TILE]
        out[part] = new.astype(out.dtype)


def update_chunk(factor, contrib, scalars, chunk, width, groups):
    parts = 4 if groups % 4 == 0 else 1
    depth = factor.shape[1]
    block = min(width, 1024)
    steps = width // block
    tiles = factor.reshape(-1, TILE, depth)
    left_specs = [
        pl.BlockSpec(
            (1, TILE, depth),
            lambda n, m, s, part=part: (s[groups] + s[m * parts + part], 0, 0),
        )
        for part in range(parts)
    ]
    right_spec = pl.BlockSpec(
        (block, depth), lambda n, m, s: (s[groups + 1] + chunk * steps + n, 0)
    )
    old_specs = [
        pl.BlockSpec(
            (TILE, block), lambda n, m, s, part=part: (s[m * parts + part], chunk * steps + n)
        )
        for part in range(parts)
    ]
    return pl.pallas_call(
        lambda *refs: update_kernel(parts, *refs),
        out_shape=jax.ShapeDtypeStruct((groups, TILE, width), contrib.dtype),
        grid_spec=pltpu.PrefetchScalarGridSpec(
            num_scalar_prefetch=1,
            grid=(steps, groups // parts),
            in_specs=left_specs + [right_spec] + old_specs,
            out_specs=pl.BlockSpec((parts, TILE, block), lambda n, m, s: (m, 0, n)),
        ),
        name="update",
    )(scalars, *([tiles] * parts), factor, *([contrib] * parts))


def assemble(row_code, col_code, has_cross, recv, near, far, cross_recv, cross_near, init, block):
    fronts, per_rows = row_code.shape
    per_cols = col_code.shape[1]
    chunks = len(recv)
    width = recv[0].shape[2]
    span = chunks * width
    cross_span = cross_recv.shape[2]
    vectors = block.shape[1]
    cap = recv[0].shape[0]
    scalars = jnp.concatenate(
        [row_code.reshape(-1), col_code.reshape(-1), has_cross.astype(jnp.int32).reshape(1)]
    )
    col_base = fronts * per_rows
    flag = col_base + fronts * per_cols

    def kernel(s, *refs):
        recv_refs = refs[:chunks]
        near_refs = refs[chunks : 2 * chunks]
        far_ref, cross_recv_ref, cross_near_ref, init_ref, block_ref = refs[
            2 * chunks : 2 * chunks + 5
        ]
        schur_ref, product_ref = refs[2 * chunks + 5 : 2 * chunks + 7]
        held, rounded, sems = refs[2 * chunks + 7 :]
        step = pl.program_id(0)

        def moves(b, act):
            slot = b % 2
            for f in range(fronts):
                code = s[f * per_rows + b]
                index = code % cap

                def go(source, place, lanes, which):
                    act(
                        pltpu.make_async_copy(
                            source.at[index],
                            held.at[slot, f, :, pl.ds(place, lanes)],
                            sems.at[slot, f, which],
                        )
                    )

                @pl.when((code >= 0) & (code < cap))
                def _():
                    for chunk in range(chunks):
                        go(recv_refs[chunk], chunk * width, width, chunk)

                    @pl.when(s[flag] > 0)
                    def _():
                        go(cross_recv_ref, span, cross_span, chunks)

                @pl.when((code >= cap) & (code < 2 * cap))
                def _():
                    for chunk in range(chunks):
                        go(near_refs[chunk], chunk * width, width, chunk)

                    @pl.when(s[flag] > 0)
                    def _():
                        go(cross_near_ref, span, cross_span, chunks)

                @pl.when(code >= 2 * cap)
                def _():
                    go(far_ref, 0, span + cross_span, chunks)

        @pl.when(step == 0)
        def _():
            moves(step, lambda copy: copy.start())

        @pl.when(step + 1 < per_rows)
        def _():
            moves(step + 1, lambda copy: copy.start())

        moves(step, lambda copy: copy.wait())
        slot = step % 2

        def column(c, carry):
            lanes = pl.ds(pl.multiple_of(c * TILE, TILE), TILE)
            total = init_ref[:, lanes].astype(jnp.float32)
            for f in range(fronts):
                code = s[col_base + f * per_cols + c]
                used = (code >= 0) & (s[f * per_rows + step] >= 0)
                place = pl.multiple_of(jnp.maximum(code, 0) * TILE, TILE)
                piece = held[slot, f, :, pl.ds(place, TILE)].astype(jnp.float32)
                total = total + jnp.where(used, piece, 0.0)
            schur_ref[:, lanes] = total
            rounded[:, lanes] = total.astype(jnp.bfloat16)
            return carry

        lax.fori_loop(0, per_cols, column, 0, unroll=4 if per_cols % 4 == 0 else 1)
        product_ref[...] = jnp.dot(
            rounded[...], block_ref[...], preferred_element_type=jnp.float32
        )

    anywhere = pl.BlockSpec(memory_space=pl.ANY)
    wide = per_cols * TILE
    return pl.pallas_call(
        kernel,
        out_shape=(
            jax.ShapeDtypeStruct((per_rows * TILE, wide), jnp.float32),
            jax.ShapeDtypeStruct((per_rows * TILE, vectors), jnp.float32),
        ),
        grid_spec=pltpu.PrefetchScalarGridSpec(
            num_scalar_prefetch=1,
            grid=(per_rows,),
            in_specs=[anywhere] * (2 * chunks + 3)
            + [
                pl.BlockSpec((TILE, wide), lambda b, s: (b, 0)),
                pl.BlockSpec((wide, vectors), lambda b, s: (0, 0)),
            ],
            out_specs=[
                pl.BlockSpec((TILE, wide), lambda b, s: (b, 0)),
                pl.BlockSpec((TILE, vectors), lambda b, s: (b, 0)),
            ],
            scratch_shapes=[
                pltpu.VMEM((2, fronts, TILE, span + cross_span), jnp.bfloat16),
                pltpu.VMEM((TILE, wide), jnp.bfloat16),
                pltpu.SemaphoreType.DMA((2, fronts, chunks + 1)),
            ],
        ),
        name="assemble",
    )(scalars, *recv, *near, far, cross_recv, cross_near, init, block)


def shards(pivot_block, border, contrib, inverses, row_tiles, col_tiles, owner, schur_init, block):
    n_front = lax.axis_size("front")
    n_row = lax.axis_size("row")
    n_col = lax.axis_size("col")
    front_index = lax.axis_index("front")
    row_index = lax.axis_index("row")
    col_index = lax.axis_index("col")
    groups = n_front * n_row
    tiles_all = row_tiles.shape[1]
    slots_all = owner.shape[0]
    row_span = border.shape[1]
    col_span = contrib.shape[2]
    tile_rows = row_span // TILE
    tile_cols = col_span // TILE
    rows_per_group = slots_all // groups
    cols_per_group = slots_all // n_col
    share = row_span // n_col
    chunks = CHUNKS if tile_cols % CHUNKS == 0 else 1
    width = col_span // chunks
    me = front_index * n_row + row_index

    own_rows = lax.dynamic_slice_in_dim(border[0], col_index * share, share, 0)
    leaves = eliminate(pivot_block[0], own_rows, inverses[0])
    factor = lax.all_gather(leaves, ("row", "col"), axis=0, tiled=True)

    slot_rows = owner[row_tiles].reshape(groups, tile_rows)
    plan = row_plan(slot_rows, rows_per_group, groups, ADJACENT)
    held = lambda table: lax.dynamic_index_in_dim(table, me, 1, keepdims=False)
    my_group = held(plan["to_group"])
    my_order = held(plan["order"])
    near_index = jnp.sum(
        (held(plan["near"])[None, :] & (my_order[None, :] == jnp.arange(ADJACENT)[:, None])).astype(
            jnp.int32
        )
        * jnp.arange(groups),
        axis=-1,
    )
    for_me = plan["to_group"] == me
    code = jnp.where(
        ~plan["astray"],
        jnp.arange(groups)[:, None],
        jnp.where(plan["near"], groups + plan["order"], 2 * groups + plan["far_place"]),
    )
    hit = for_me[:, :, None] & (plan["to_within"][:, :, None] == jnp.arange(rows_per_group))
    row_code = (
        jnp.sum(
            jnp.where(hit, code[:, :, None] + 1, 0).reshape(
                n_front, n_row * groups, rows_per_group
            ),
            axis=1,
        )
        - 1
    )

    slot_cols = owner[col_tiles].reshape(n_front, n_col, tile_cols)
    to_col = slot_cols // cols_per_group
    within_col = slot_cols % cols_per_group
    crossing = to_col != jnp.arange(n_col)[None, :, None]
    cross_order = count(
        (to_col[..., :, None] == to_col[..., None, :]) & earlier(tile_cols)[None, None]
    )
    cross_rounds = jnp.max(jnp.where(crossing, cross_order + 1, 0))
    flat_to = to_col.reshape(n_front, -1)
    flat_cross = crossing.reshape(n_front, -1)
    cross_place = count(
        (flat_to[:, :, None] == flat_to[:, None, :])
        & flat_cross[:, None, :]
        & earlier(n_col * tile_cols)[None]
    ).reshape(n_front, n_col, tile_cols)
    col_place = jnp.where(crossing, tile_cols + cross_place, jnp.arange(tile_cols))
    col_hit = (to_col == col_index)[..., None] & (
        within_col[..., None] == jnp.arange(cols_per_group)
    )
    col_code = jnp.sum(jnp.where(col_hit, col_place[..., None] + 1, 0), axis=(1, 2)) - 1
    my_to = to_col[front_index]
    my_cross_order = cross_order[front_index]
    my_cross_place = cross_place[front_index]

    scalars = jnp.concatenate(
        [
            lax.dynamic_index_in_dim(plan["source_row"], me, 0, keepdims=False),
            jnp.stack([row_index * tile_rows, col_index * (col_span // min(width, 1024))]),
        ]
    ).astype(jnp.int32)
    neighbours = [(g, g ^ 1) for g in range(groups)]

    def settle(received):
        picked = jnp.take(received, near_index, axis=0)
        return lax.ppermute(picked, FR, neighbours)

    sent, recv, near = [], [], []
    for chunk in range(chunks):
        piece = update_chunk(factor, contrib[0], scalars, chunk, width, groups)
        sent.append(piece)
        recv.append(lax.all_to_all(piece, FR, split_axis=0, concat_axis=0, tiled=True))
    for chunk in range(chunks):
        near.append(settle(recv[chunk]))

    cross_span = (tile_cols + 1) * TILE

    def cross_round(state):
        turn, buffer = state
        picks = []
        for other in range(n_col):
            chosen = (my_to[col_index] == other) & (my_cross_order[col_index] == turn)
            column = jnp.sum(chosen.astype(jnp.int32) * jnp.arange(tile_cols))
            pick = None
            for chunk in range(chunks):
                local = column - chunk * (width // TILE)
                inside = (local >= 0) & (local < width // TILE)
                part = lax.dynamic_slice_in_dim(
                    sent[chunk], jnp.clip(local, 0, width // TILE - 1) * TILE, TILE, 2
                )
                pick = part if pick is None else jnp.where(inside, part, pick)
            picks.append(pick)
        arrived = lax.all_to_all(jnp.stack(picks), "col", split_axis=0, concat_axis=0, tiled=True)
        for other in range(n_col):
            chosen = (
                (my_to[other] == col_index) & (my_cross_order[other] == turn) & (other != col_index)
            )
            place = jnp.where(
                jnp.any(chosen),
                jnp.sum(jnp.where(chosen, my_cross_place[other], 0)),
                tile_cols,
            )
            buffer = lax.dynamic_update_slice_in_dim(buffer, arrived[other], place * TILE, 2)
        return (turn + 1, buffer)

    crossed = unwritten((groups, TILE, cross_span), contrib.dtype)
    _, crossed = lax.while_loop(
        lambda state: state[0] < cross_rounds, cross_round, (jnp.int32(0), crossed)
    )

    def cross_exchange(state):
        received = lax.all_to_all(crossed, FR, split_axis=0, concat_axis=0, tiled=True)
        return (state[0] + 1, received, settle(received))

    _, cross_recv, cross_near = lax.while_loop(
        lambda state: state[0] < jnp.minimum(cross_rounds, 1),
        cross_exchange,
        (
            jnp.int32(0),
            unwritten((groups, TILE, cross_span), contrib.dtype),
            unwritten((ADJACENT, TILE, cross_span), contrib.dtype),
        ),
    )

    my_far = held(plan["far"])
    my_far_round = held(plan["far_round"])

    def far_exchange(state):
        turn, buffer = state
        chosen = (
            my_far[None, :]
            & (my_far_round[None, :] == turn)
            & (my_group[None, :] == jnp.arange(groups)[:, None])
        )
        index = jnp.sum(chosen.astype(jnp.int32) * jnp.arange(groups), axis=-1)
        rows = jnp.concatenate(
            [jnp.take(part, index, axis=0) for part in recv + [cross_recv]], axis=2
        )
        arrived = lax.all_to_all(rows, FR, split_axis=0, concat_axis=0, tiled=True)
        coming = plan["far"] & for_me & (plan["far_round"] == turn)
        place = jnp.where(
            jnp.any(coming, axis=0),
            jnp.sum(jnp.where(coming, plan["far_place"], 0), axis=0),
            groups,
        )
        for holder in range(groups):
            buffer = lax.dynamic_update_slice_in_dim(
                buffer, arrived[holder : holder + 1], place[holder], 0
            )
        return (turn + 1, buffer)

    far = unwritten((groups + 1, TILE, col_span + cross_span), contrib.dtype)
    _, far = lax.while_loop(
        lambda state: state[0] < plan["rounds"], far_exchange, (jnp.int32(0), far)
    )

    schur, partial = assemble(
        row_code,
        col_code,
        cross_rounds > 0,
        recv,
        near,
        far,
        cross_recv,
        cross_near,
        schur_init,
        block,
    )
    if n_col == 2:
        part = partial.shape[0] // n_col
        keep = lax.dynamic_slice_in_dim(partial, col_index * part, part, 0)
        give = lax.dynamic_slice_in_dim(partial, (1 - col_index) * part, part, 0)
        product = keep + lax.ppermute(give, "col", [(0, 1), (1, 0)])
    else:
        product = lax.psum_scatter(partial, "col", scatter_dimension=0, tiled=True)
    return (schur, product)


def solution(mesh):
    in_specs = (
        P("front", None, None),
        P("front", "row", None),
        P("front", "row", "col"),
        P("front", None, None, None),
        P(),
        P(),
        P(),
        P(("front", "row"), "col"),
        P("col", None),
    )
    out_specs = (P(("front", "row"), "col"), P(("front", "row", "col"), None))
    return jax.shard_map(shards, mesh=mesh, in_specs=in_specs, out_specs=out_specs, check_vma=False)
```

```python
import jax
import jax.numpy as jnp
from jax import lax
from jax.experimental import pallas as pl
from jax.experimental.pallas import tpu as pltpu
from jax.sharding import PartitionSpec as P


TILE = 128
CHUNKS = 4
ADJACENT = 8
FR = ("front", "row")


def pivot_kernel(pivot, inverse_set, out):
    panels, width, _ = inverse_set.shape
    now = {
        (i, j): pivot[i * width : (i + 1) * width, j * width : (j + 1) * width].astype(jnp.float32)
        for i in range(panels)
        for j in range(i + 1)
    }
    out[...] = jnp.zeros_like(out)
    for k in range(panels - 1):
        lower = {}
        for i in range(k + 1, panels):
            lower[i] = jnp.dot(
                now[i, k].astype(jnp.bfloat16), inverse_set[k], preferred_element_type=jnp.float32
            ).astype(jnp.bfloat16)
            out[k, i * width : (i + 1) * width, :] = lower[i]
        for i in range(k + 1, panels):
            for j in range(k + 1, i + 1):
                now[i, j] = now[i, j] - lax.dot_general(
                    lower[i], lower[j], (((1,), (1,)), ((), ())), preferred_element_type=jnp.float32
                )


def pivot_panels(pivot, inverse_set):
    panels, width, _ = inverse_set.shape
    return pl.pallas_call(
        pivot_kernel,
        out_shape=jax.ShapeDtypeStruct((panels, pivot.shape[0], width), jnp.bfloat16),
        name="pivot",
    )(pivot, inverse_set)


def rows_kernel(rows, inverse_set, lower, out):
    panels, width, _ = inverse_set.shape
    now = [rows[:, j * width : (j + 1) * width].astype(jnp.float32) for j in range(panels)]
    for k in range(panels):
        side = jnp.dot(
            now[k].astype(jnp.bfloat16), inverse_set[k], preferred_element_type=jnp.float32
        ).astype(jnp.bfloat16)
        out[:, k * width : (k + 1) * width] = side
        for j in range(k + 1, panels):
            now[j] = now[j] - lax.dot_general(
                side,
                lower[k, j * width : (j + 1) * width, :],
                (((1,), (1,)), ((), ())),
                preferred_element_type=jnp.float32,
            )


def eliminate(rows, inverse_set, lower):
    size, depth = rows.shape
    step = min(size, 512)
    return pl.pallas_call(
        rows_kernel,
        out_shape=jax.ShapeDtypeStruct(rows.shape, jnp.bfloat16),
        grid=(size // step,),
        in_specs=[
            pl.BlockSpec((step, depth), lambda i: (i, 0)),
            pl.BlockSpec(inverse_set.shape, lambda i: (0, 0, 0)),
            pl.BlockSpec(lower.shape, lambda i: (0, 0, 0)),
        ],
        out_specs=pl.BlockSpec((step, depth), lambda i: (i, 0)),
        name="eliminate",
    )(rows, inverse_set, lower)


def collect_border(own, row_index, col_index):
    n_row = 4
    half = own.shape[0] // 2
    up = [(z, z + 1) for z in range(n_row - 1)]
    down = [(z + 1, z) for z in range(n_row - 1)]
    piece = lax.dynamic_slice_in_dim(own, col_index * half, half, 0)
    rest = lax.dynamic_slice_in_dim(own, (1 - col_index) * half, half, 0)
    below, above = [piece], [piece]

    def by_row(options):
        chosen = options[0]
        for z in range(1, n_row):
            chosen = jnp.where(row_index == z, options[z], chosen)
        return chosen

    for _ in range(n_row - 1):
        below.append(lax.ppermute(below[-1], "row", up))
        above.append(lax.ppermute(above[-1], "row", down))
    held = (row_index // 2) == col_index
    near = by_row([above[2], above[1], below[1], below[2]])
    near_other = lax.ppermute(near, ("row", "col"), [(0, 1), (2, 3), (5, 4), (7, 6)])
    first = jnp.where(held, piece, near)

    def second(done):
        _, arrived = lax.optimization_barrier((done, near_other))
        return jnp.where(held, rest, arrived)

    def others(done):
        _, up_moved, down_moved = lax.optimization_barrier((done, below, above))
        low = by_row([down_moved[1], up_moved[1], up_moved[2], up_moved[3]])
        high = by_row([down_moved[3], down_moved[2], down_moved[1], up_moved[1]])
        other = lax.ppermute(jnp.where(col_index == 0, high, low), "col", [(0, 1), (1, 0)])
        return jnp.where(col_index == 0, low, high), other

    return first, second, others


def count(mask, axis=-1):
    return jnp.sum(mask.astype(jnp.int32), axis=axis)


def earlier(n):
    return jnp.arange(n)[None, :] < jnp.arange(n)[:, None]


def row_plan(slot_rows, per_group, groups, adjacent):
    sources, tile_rows = slot_rows.shape
    target = slot_rows // per_group
    within = slot_rows % per_group
    same = target[:, :, None] == target[:, None, :]
    rank = count(same & earlier(tile_rows)[None])
    extra = rank > 0
    key = target * tile_rows + rank
    extra_order = count(extra[:, None, :] & (key[:, None, :] < key[:, :, None]))
    empty = count(target[:, None, :] == jnp.arange(groups)[None, :, None]) == 0
    empty_order = count(empty[:, None, :] & earlier(groups)[None])
    lands = jnp.where(
        extra[:, None, :],
        empty[:, :, None] & (empty_order[:, :, None] == extra_order[:, None, :]),
        target[:, None, :] == jnp.arange(groups)[None, :, None],
    ).astype(jnp.int32)
    source_row = jnp.sum(lands * jnp.arange(tile_rows), axis=-1)
    to_group = jnp.sum(lands * target[:, None, :], axis=-1)
    to_within = jnp.sum(lands * within[:, None, :], axis=-1)
    here = jnp.arange(groups)[None, :]
    astray = to_group != here
    order = count(
        (to_group[:, None, :] == to_group[None, :, :])
        & astray[None]
        & earlier(sources)[:, :, None],
        axis=1,
    )
    near = astray & (to_group == (here ^ 1)) & (order < adjacent)
    far = astray & ~near
    far_round = jnp.where(to_group == (here ^ 1), order - adjacent, order)
    rounds = jnp.max(jnp.where(far, far_round + 1, 0))
    flat_group = to_group.T.reshape(-1)
    flat_far = far.T.reshape(-1)
    total = flat_group.shape[0]
    far_place = count(
        (flat_group[None, :] == flat_group[:, None]) & flat_far[None, :] & earlier(total)
    ).reshape(groups, sources).T
    return dict(
        source_row=source_row,
        to_group=to_group,
        to_within=to_within,
        order=order,
        near=near,
        far=far,
        far_round=far_round,
        far_place=far_place,
        astray=astray,
        rounds=rounds,
    )


def unwritten(shape, dtype):
    return pl.pallas_call(
        lambda out: None,
        out_shape=jax.ShapeDtypeStruct(shape, dtype),
        out_specs=pl.BlockSpec(memory_space=pl.ANY),
    )()


def update_kernel(parts, scalars, *refs):
    left = refs[:parts]
    right = refs[parts]
    old = refs[parts + 1 : 2 * parts + 1]
    out = refs[2 * parts + 1]
    lhs = jnp.concatenate([part[0] for part in left], axis=0)
    change = lax.dot_general(
        lhs, right[...], (((1,), (1,)), ((), ())), preferred_element_type=jnp.float32
    )
    for part in range(parts):
        new = old[part][...].astype(jnp.float32) - change[part * TILE : (part + 1) * TILE]
        out[part] = new.astype(out.dtype)


def update_chunk(mine, theirs, first, contrib, scalars, chunk, width, groups):
    parts = 4 if groups % 4 == 0 else 1
    depth = mine.shape[1]
    block = min(width, 1024)
    steps = width // block
    tiles = mine.reshape(-1, TILE, depth)
    left_specs = [
        pl.BlockSpec((1, TILE, depth), lambda n, m, s, part=part: (s[m * parts + part], 0, 0))
        for part in range(parts)
    ]
    right_spec = pl.BlockSpec((block, depth), lambda n, m, s: (first // block + n, 0))
    old_specs = [
        pl.BlockSpec(
            (TILE, block),
            lambda n, m, s, part=part: (s[m * parts + part], s[groups + chunk] // block + n),
        )
        for part in range(parts)
    ]
    return pl.pallas_call(
        lambda *refs: update_kernel(parts, *refs),
        out_shape=jax.ShapeDtypeStruct((groups, TILE, width), contrib.dtype),
        grid_spec=pltpu.PrefetchScalarGridSpec(
            num_scalar_prefetch=1,
            grid=(steps, groups // parts),
            in_specs=left_specs + [right_spec] + old_specs,
            out_specs=pl.BlockSpec((parts, TILE, block), lambda n, m, s: (m, 0, n)),
        ),
        name="update",
    )(scalars, *([tiles] * parts), theirs, *([contrib] * parts))


def assemble(row_code, row_from, starts, col_code, has_cross, recv, near, far, cross_recv, cross_near, init, block):
    fronts, per_rows = row_code.shape
    per_cols = col_code.shape[1]
    chunks = len(recv)
    width = recv[0].shape[2]
    span = chunks * width
    cross_span = cross_recv.shape[2]
    vectors = block.shape[1]
    cap = recv[0].shape[0]
    scalars = jnp.concatenate(
        [
            row_code.reshape(-1),
            col_code.reshape(-1),
            has_cross.astype(jnp.int32).reshape(1),
            row_from.reshape(-1),
            starts.reshape(-1),
        ]
    ).astype(jnp.int32)
    col_base = fronts * per_rows
    flag = col_base + fronts * per_cols
    from_base = flag + 1
    start_base = from_base + fronts * per_rows

    def kernel(s, *refs):
        recv_refs = refs[:chunks]
        near_refs = refs[chunks : 2 * chunks]
        far_ref, cross_recv_ref, cross_near_ref, init_ref, block_ref = refs[
            2 * chunks : 2 * chunks + 5
        ]
        schur_ref, product_ref = refs[2 * chunks + 5 : 2 * chunks + 7]
        held, rounded, sems = refs[2 * chunks + 7 :]
        step = pl.program_id(0)

        def moves(b, act):
            slot = b % 2
            for f in range(fronts):
                code = s[f * per_rows + b]
                index = code % cap
                source_row = s[from_base + f * per_rows + b]
                places = [
                    pl.multiple_of(s[start_base + source_row * chunks + chunk], TILE)
                    for chunk in range(chunks)
                ]

                def go(source, place, lanes, which, offset=None):
                    act(
                        pltpu.make_async_copy(
                            source.at[index]
                            if offset is None
                            else source.at[index, :, pl.ds(offset, lanes)],
                            held.at[slot, f, :, pl.ds(place, lanes)],
                            sems.at[slot, f, which],
                        )
                    )

                @pl.when((code >= 0) & (code < cap))
                def _():
                    for chunk in range(chunks):
                        go(recv_refs[chunk], places[chunk], width, chunk)

                    @pl.when(s[flag] > 0)
                    def _():
                        go(cross_recv_ref, span, cross_span, chunks)

                @pl.when((code >= cap) & (code < 2 * cap))
                def _():
                    for chunk in range(chunks):
                        go(near_refs[chunk], places[chunk], width, chunk)

                    @pl.when(s[flag] > 0)
                    def _():
                        go(cross_near_ref, span, cross_span, chunks)

                @pl.when(code >= 2 * cap)
                def _():
                    for chunk in range(chunks):
                        go(far_ref, places[chunk], width, chunk, chunk * width)

                    @pl.when(s[flag] > 0)
                    def _():
                        go(far_ref, span, cross_span, chunks, span)

        @pl.when(step == 0)
        def _():
            moves(step, lambda copy: copy.start())

        @pl.when(step + 1 < per_rows)
        def _():
            moves(step + 1, lambda copy: copy.start())

        moves(step, lambda copy: copy.wait())
        slot = step % 2

        def column(c, carry):
            lanes = pl.ds(pl.multiple_of(c * TILE, TILE), TILE)
            total = init_ref[:, lanes].astype(jnp.float32)
            for f in range(fronts):
                code = s[col_base + f * per_cols + c]
                used = (code >= 0) & (s[f * per_rows + step] >= 0)
                place = pl.multiple_of(jnp.maximum(code, 0) * TILE, TILE)
                piece = held[slot, f, :, pl.ds(place, TILE)].astype(jnp.float32)
                total = total + jnp.where(used, piece, 0.0)
            schur_ref[:, lanes] = total
            rounded[:, lanes] = total.astype(jnp.bfloat16)
            return carry

        lax.fori_loop(0, per_cols, column, 0, unroll=2)
        product_ref[...] = jnp.dot(
            rounded[...], block_ref[...], preferred_element_type=jnp.float32
        )

    anywhere = pl.BlockSpec(memory_space=pl.ANY)
    wide = per_cols * TILE
    return pl.pallas_call(
        kernel,
        out_shape=(
            jax.ShapeDtypeStruct((per_rows * TILE, wide), jnp.float32),
            jax.ShapeDtypeStruct((per_rows * TILE, vectors), jnp.float32),
        ),
        grid_spec=pltpu.PrefetchScalarGridSpec(
            num_scalar_prefetch=1,
            grid=(per_rows,),
            in_specs=[anywhere] * (2 * chunks + 3)
            + [
                pl.BlockSpec((TILE, wide), lambda b, s: (b, 0)),
                pl.BlockSpec((wide, vectors), lambda b, s: (0, 0)),
            ],
            out_specs=[
                pl.BlockSpec((TILE, wide), lambda b, s: (b, 0)),
                pl.BlockSpec((TILE, vectors), lambda b, s: (b, 0)),
            ],
            scratch_shapes=[
                pltpu.VMEM((2, fronts, TILE, span + cross_span), jnp.bfloat16),
                pltpu.VMEM((TILE, wide), jnp.bfloat16),
                pltpu.SemaphoreType.DMA((2, fronts, chunks + 1)),
            ],
        ),
        name="assemble",
    )(scalars, *recv, *near, far, cross_recv, cross_near, init, block)


def shards(pivot_block, border, contrib, inverses, row_tiles, col_tiles, owner, schur_init, block):
    n_front = lax.axis_size("front")
    n_row = lax.axis_size("row")
    n_col = lax.axis_size("col")
    front_index = lax.axis_index("front")
    row_index = lax.axis_index("row")
    col_index = lax.axis_index("col")
    groups = n_front * n_row
    slots_all = owner.shape[0]
    row_span = border.shape[1]
    col_span = contrib.shape[2]
    tile_rows = row_span // TILE
    tile_cols = col_span // TILE
    rows_per_group = slots_all // groups
    cols_per_group = slots_all // n_col
    chunks = CHUNKS if tile_cols % CHUNKS == 0 else 1
    width = col_span // chunks
    me = front_index * n_row + row_index

    lower = pivot_panels(pivot_block[0], inverses[0])
    mine = eliminate(border[0], inverses[0], lower)
    if n_row == 4 and n_col == 2 and col_span == 2 * row_span and chunks == 4:
        first, second, others = collect_border(border[0], row_index, col_index)
        theirs = [eliminate(first, inverses[0], lower)]
        lines = jnp.arange(n_row)
        turned = jnp.where(col_index == 0, lines > 0, lines == n_row - 1).astype(jnp.int32)
        starts = width * jnp.stack(
            [
                2 * turned + col_index,
                2 * turned + 1 - col_index,
                2 - 2 * turned + col_index,
                3 - 2 * turned - col_index,
            ],
            axis=1,
        )
    else:
        share = row_span // n_col
        own_rows = lax.dynamic_slice_in_dim(mine, col_index * share, share, 0)
        factor = lax.all_gather(own_rows, ("row", "col"), axis=0, tiled=True)
        theirs = [lax.dynamic_slice_in_dim(factor, col_index * col_span, col_span, 0)]
        second = None
        starts = jnp.broadcast_to(jnp.arange(chunks) * width, (n_row, chunks))
    my_starts = lax.dynamic_index_in_dim(starts, row_index, 0, keepdims=False)

    slot_rows = owner[row_tiles].reshape(groups, tile_rows)
    plan = row_plan(slot_rows, rows_per_group, groups, ADJACENT)
    held = lambda table: lax.dynamic_index_in_dim(table, me, 1, keepdims=False)
    my_group = held(plan["to_group"])
    my_order = held(plan["order"])
    near_index = jnp.sum(
        (held(plan["near"])[None, :] & (my_order[None, :] == jnp.arange(ADJACENT)[:, None])).astype(
            jnp.int32
        )
        * jnp.arange(groups),
        axis=-1,
    )
    for_me = plan["to_group"] == me
    code = jnp.where(
        ~plan["astray"],
        jnp.arange(groups)[:, None],
        jnp.where(plan["near"], groups + plan["order"], 2 * groups + plan["far_place"]),
    )
    hit = for_me[:, :, None] & (plan["to_within"][:, :, None] == jnp.arange(rows_per_group))
    row_code = (
        jnp.sum(
            jnp.where(hit, code[:, :, None] + 1, 0).reshape(
                n_front, n_row * groups, rows_per_group
            ),
            axis=1,
        )
        - 1
    )

    row_from = jnp.sum(
        jnp.where(hit, (jnp.arange(groups) % n_row)[:, None, None], 0).reshape(
            n_front, n_row * groups, rows_per_group
        ),
        axis=1,
    )

    slot_cols = owner[col_tiles].reshape(n_front, n_col, tile_cols)
    to_col = slot_cols // cols_per_group
    within_col = slot_cols % cols_per_group
    crossing = to_col != jnp.arange(n_col)[None, :, None]
    cross_order = count(
        (to_col[..., :, None] == to_col[..., None, :]) & earlier(tile_cols)[None, None]
    )
    cross_rounds = jnp.max(jnp.where(crossing, cross_order + 1, 0))
    flat_to = to_col.reshape(n_front, -1)
    flat_cross = crossing.reshape(n_front, -1)
    cross_place = count(
        (flat_to[:, :, None] == flat_to[:, None, :])
        & flat_cross[:, None, :]
        & earlier(n_col * tile_cols)[None]
    ).reshape(n_front, n_col, tile_cols)
    col_place = jnp.where(crossing, tile_cols + cross_place, jnp.arange(tile_cols))
    col_hit = (to_col == col_index)[..., None] & (
        within_col[..., None] == jnp.arange(cols_per_group)
    )
    col_code = jnp.sum(jnp.where(col_hit, col_place[..., None] + 1, 0), axis=(1, 2)) - 1
    my_to = to_col[front_index]
    my_cross_order = cross_order[front_index]
    my_cross_place = cross_place[front_index]

    scalars = jnp.concatenate(
        [
            lax.dynamic_index_in_dim(plan["source_row"], me, 0, keepdims=False),
            my_starts,
        ]
    ).astype(jnp.int32)
    neighbours = [(g, g ^ 1) for g in range(groups)]

    def settle(received):
        picked = jnp.take(received, near_index, axis=0, mode="clip")
        return picked, lax.ppermute(picked, FR, neighbours)

    sent, recv, near, picks = [], [], [], []
    for chunk in range(chunks):
        per_part = chunks if second is None else 1
        piece = update_chunk(
            mine,
            theirs[chunk // per_part],
            (chunk % per_part) * width,
            contrib[0],
            scalars,
            chunk,
            width,
            groups,
        )
        if chunk == 0 and second is not None:
            theirs.append(eliminate(second(piece), inverses[0], lower))
            theirs += [eliminate(part, inverses[0], lower) for part in others(theirs[1])]
        if chunk >= 2:
            piece, picks[chunk - 2] = lax.optimization_barrier((piece, picks[chunk - 2]))
        sent.append(piece)
        recv.append(lax.all_to_all(piece, FR, split_axis=0, concat_axis=0, tiled=True))
        picked, moved = settle(recv[chunk])
        picks.append(picked)
        near.append(moved)

    cross_span = (tile_cols + 1) * TILE

    def cross_round(state):
        turn, buffer = state
        picks = []
        for other in range(n_col):
            chosen = (my_to[col_index] == other) & (my_cross_order[col_index] == turn)
            column = jnp.sum(chosen.astype(jnp.int32) * jnp.arange(tile_cols))
            pick = None
            for chunk in range(chunks):
                local = column - my_starts[chunk] // TILE
                inside = (local >= 0) & (local < width // TILE)
                part = lax.dynamic_slice_in_dim(
                    sent[chunk], jnp.clip(local, 0, width // TILE - 1) * TILE, TILE, 2
                )
                pick = part if pick is None else jnp.where(inside, part, pick)
            picks.append(pick)
        arrived = lax.all_to_all(jnp.stack(picks), "col", split_axis=0, concat_axis=0, tiled=True)
        for other in range(n_col):
            chosen = (
                (my_to[other] == col_index) & (my_cross_order[other] == turn) & (other != col_index)
            )
            place = jnp.where(
                jnp.any(chosen),
                jnp.sum(jnp.where(chosen, my_cross_place[other], 0)),
                tile_cols,
            )
            buffer = lax.dynamic_update_slice_in_dim(buffer, arrived[other], place * TILE, 2)
        return (turn + 1, buffer)

    cross_rounds, _ = lax.optimization_barrier((cross_rounds, recv[-1]))
    far_rounds, _ = lax.optimization_barrier((plan["rounds"], recv[-1]))
    crossed = unwritten((groups, TILE, cross_span), contrib.dtype)
    _, crossed = lax.while_loop(
        lambda state: state[0] < cross_rounds, cross_round, (jnp.int32(0), crossed)
    )

    def cross_exchange(state):
        mark = jnp.full((1, 1, TILE), state[0], contrib.dtype)
        outgoing = lax.dynamic_update_slice(state[1], mark, (0, 0, tile_cols * TILE))
        received = lax.all_to_all(outgoing, FR, split_axis=0, concat_axis=0, tiled=True)
        return (cross_rounds, outgoing, received, settle(received)[1])

    _, _, cross_recv, cross_near = lax.while_loop(
        lambda state: state[0] < cross_rounds,
        cross_exchange,
        (
            jnp.int32(0),
            crossed,
            unwritten((groups, TILE, cross_span), contrib.dtype),
            unwritten((ADJACENT, TILE, cross_span), contrib.dtype),
        ),
    )

    my_far = held(plan["far"])
    my_far_round = held(plan["far_round"])

    def far_exchange(state):
        turn, buffer = state
        chosen = (
            my_far[None, :]
            & (my_far_round[None, :] == turn)
            & (my_group[None, :] == jnp.arange(groups)[:, None])
        )
        index = jnp.sum(chosen.astype(jnp.int32) * jnp.arange(groups), axis=-1)
        rows = jnp.concatenate(
            [jnp.take(part, index, axis=0, mode="clip") for part in recv + [cross_recv]], axis=2
        )
        arrived = lax.all_to_all(rows, FR, split_axis=0, concat_axis=0, tiled=True)
        coming = plan["far"] & for_me & (plan["far_round"] == turn)
        place = jnp.where(
            jnp.any(coming, axis=0),
            jnp.sum(jnp.where(coming, plan["far_place"], 0), axis=0),
            groups,
        )
        for holder in range(groups):
            buffer = lax.dynamic_update_slice_in_dim(
                buffer, arrived[holder : holder + 1], place[holder], 0
            )
        return (turn + 1, buffer)

    far = unwritten((groups + 1, TILE, col_span + cross_span), contrib.dtype)
    _, far = lax.while_loop(
        lambda state: state[0] < far_rounds, far_exchange, (jnp.int32(0), far)
    )

    schur, partial = assemble(
        row_code,
        row_from,
        starts,
        col_code,
        cross_rounds > 0,
        recv,
        near,
        far,
        cross_recv,
        cross_near,
        schur_init,
        block,
    )
    if n_col == 2:
        part = partial.shape[0] // n_col
        keep = lax.dynamic_slice_in_dim(partial, col_index * part, part, 0)
        give = lax.dynamic_slice_in_dim(partial, (1 - col_index) * part, part, 0)
        product = keep + lax.ppermute(give, "col", [(0, 1), (1, 0)])
    else:
        product = lax.psum_scatter(partial, "col", scatter_dimension=0, tiled=True)
    return (schur, product)


def solution(mesh):
    in_specs = (
        P("front", None, None),
        P("front", "row", None),
        P("front", "row", "col"),
        P("front", None, None, None),
        P(),
        P(),
        P(),
        P(("front", "row"), "col"),
        P("col", None),
    )
    out_specs = (P(("front", "row"), "col"), P(("front", "row", "col"), None))

    return jax.shard_map(shards, mesh=mesh, in_specs=in_specs, out_specs=out_specs, check_vma=False)
```

```python
import jax
import jax.numpy as jnp
from jax import lax
from jax.experimental import pallas as pl
from jax.experimental.pallas import tpu as pltpu
from jax.sharding import PartitionSpec as P


TILE = 128
CHUNKS = 4
ROW_CAP = 6
FRONT_CAPS = (6, 4, 3)
FR = ("front", "row")


def pivot_kernel(pivot, inverse_set, out):
    panels, width, _ = inverse_set.shape
    now = {
        (i, j): pivot[i * width : (i + 1) * width, j * width : (j + 1) * width].astype(jnp.float32)
        for i in range(panels)
        for j in range(i + 1)
    }
    out[...] = jnp.zeros_like(out)
    for k in range(panels - 1):
        lower = {}
        for i in range(k + 1, panels):
            lower[i] = jnp.dot(
                now[i, k].astype(jnp.bfloat16), inverse_set[k], preferred_element_type=jnp.float32
            ).astype(jnp.bfloat16)
            out[k, i * width : (i + 1) * width, :] = lower[i]
        for i in range(k + 1, panels):
            for j in range(k + 1, i + 1):
                now[i, j] = now[i, j] - lax.dot_general(
                    lower[i], lower[j], (((1,), (1,)), ((), ())), preferred_element_type=jnp.float32
                )


def pivot_panels(pivot, inverse_set):
    panels, width, _ = inverse_set.shape
    return pl.pallas_call(
        pivot_kernel,
        out_shape=jax.ShapeDtypeStruct((panels, pivot.shape[0], width), jnp.bfloat16),
        name="pivot",
    )(pivot, inverse_set)


def rows_kernel(rows, inverse_set, lower, out):
    panels, width, _ = inverse_set.shape
    now = [rows[:, j * width : (j + 1) * width].astype(jnp.float32) for j in range(panels)]
    for k in range(panels):
        side = jnp.dot(
            now[k].astype(jnp.bfloat16), inverse_set[k], preferred_element_type=jnp.float32
        ).astype(jnp.bfloat16)
        out[:, k * width : (k + 1) * width] = side
        for j in range(k + 1, panels):
            now[j] = now[j] - lax.dot_general(
                side,
                lower[k, j * width : (j + 1) * width, :],
                (((1,), (1,)), ((), ())),
                preferred_element_type=jnp.float32,
            )


def eliminate(rows, inverse_set, lower):
    size, depth = rows.shape
    step = min(size, 512)
    return pl.pallas_call(
        rows_kernel,
        out_shape=jax.ShapeDtypeStruct(rows.shape, jnp.bfloat16),
        grid=(size // step,),
        in_specs=[
            pl.BlockSpec((step, depth), lambda i: (i, 0)),
            pl.BlockSpec(inverse_set.shape, lambda i: (0, 0, 0)),
            pl.BlockSpec(lower.shape, lambda i: (0, 0, 0)),
        ],
        out_specs=pl.BlockSpec((step, depth), lambda i: (i, 0)),
        name="eliminate",
    )(rows, inverse_set, lower)


def collect_border(own, row_index, col_index):
    n_row = 4
    half = own.shape[0] // 2
    part = half // 2
    up = [(z, z + 1) for z in range(n_row - 1)]
    down = [(z + 1, z) for z in range(n_row - 1)]
    first_row = col_index * half
    pieces = [lax.dynamic_slice_in_dim(own, first_row + p * part, part, 0) for p in range(2)]
    rest = lax.dynamic_slice_in_dim(own, half - first_row, half, 0)
    held = (row_index // 2) == col_index
    left = col_index == 0

    def by_row(options):
        chosen = options[0]
        for z in range(1, n_row):
            chosen = jnp.where(row_index == z, options[z], chosen)
        return chosen

    below = [[piece] for piece in pieces]
    above = [[piece] for piece in pieces]
    for p in range(2):
        for _ in range(n_row - 1):
            below[p].append(lax.ppermute(below[p][-1], "row", up))
            above[p].append(lax.ppermute(above[p][-1], "row", down))
    swapped = [None, None]

    def first(p, done):
        options = [above[p][2], above[p][1], below[p][1], below[p][2]]
        if done is not None:
            _, options = lax.optimization_barrier((done, options))
        near = by_row(options)
        swapped[p] = lax.ppermute(near, ("row", "col"), [(0, 1), (2, 3), (5, 4), (7, 6)])
        return jnp.where(held, pieces[p], near)

    def second(done):
        _, arrived = lax.optimization_barrier((done, swapped))
        return jnp.where(held, rest, jnp.concatenate(arrived))

    def others(done):
        _, ups, downs = lax.optimization_barrier((done, below, above))
        low = [by_row([d[1], u[1], u[2], u[3]]) for u, d in zip(ups, downs)]
        high = [by_row([d[3], d[2], d[1], u[1]]) for u, d in zip(ups, downs)]
        keep = jnp.concatenate([jnp.where(left, a, b) for a, b in zip(low, high)])
        give = jnp.concatenate([jnp.where(left, b, a) for a, b in zip(low, high)])
        other = lax.ppermute(give, "col", [(0, 1), (1, 0)])
        return keep, other

    return first, second, others


def count(mask, axis=-1):
    return jnp.sum(mask.astype(jnp.int32), axis=axis)


def earlier(n):
    return jnp.arange(n)[None, :] < jnp.arange(n)[:, None]


def row_plan(slot_rows, per_group, groups, kinds):
    sources, tile_rows = slot_rows.shape
    places = jnp.arange(groups)
    target = slot_rows // per_group
    within = slot_rows % per_group
    same = target[:, :, None] == target[:, None, :]
    extra = count(same & earlier(tile_rows)[None]) > 0
    amount = count(target[:, None, :] == places[None, :, None])
    double = amount > 1
    empty = amount == 0
    landing = jnp.zeros_like(amount)
    for step, _ in kinds[1:]:
        match = double & empty[:, places ^ step]
        landing = jnp.where(match, places ^ step, landing)
        double = double & ~match
        empty = empty & ~match[:, places ^ step]
    double_order = count(double[:, None, :] & earlier(groups)[None])
    empty_order = count(empty[:, None, :] & earlier(groups)[None])
    left = (
        double[:, :, None]
        & empty[:, None, :]
        & (double_order[:, :, None] == empty_order[:, None, :])
    )
    landing = landing + jnp.sum(left.astype(jnp.int32) * places, axis=-1)
    extra_place = jnp.sum(
        (target[:, :, None] == places).astype(jnp.int32) * landing[:, None, :], axis=-1
    )
    lands = (
        jnp.where(extra, extra_place, target)[:, None, :] == places[None, :, None]
    ).astype(jnp.int32)
    source_row = jnp.sum(lands * jnp.arange(tile_rows), axis=-1)
    to_group = jnp.sum(lands * target[:, None, :], axis=-1)
    to_within = jnp.sum(lands * within[:, None, :], axis=-1)
    here = places[None, :]
    astray = to_group != here
    order = count(
        (to_group[:, None, :] == to_group[None, :, :])
        & astray[None]
        & earlier(sources)[:, :, None],
        axis=1,
    )
    steps = to_group ^ here
    kind = jnp.zeros_like(order)
    far_round = order
    for index, (step, room) in enumerate(kinds):
        kind = jnp.where(astray & (steps == step) & (order < room), index + 1, kind)
        far_round = jnp.where(steps == step, order - room, far_round)
    far = astray & (kind == 0)
    kind = jnp.where(far, len(kinds) + 1, kind)
    rounds = jnp.max(
        jnp.where(far & (steps == places[:, None, None]), far_round + 1, 0), axis=(1, 2)
    )
    flat_group = to_group.T.reshape(-1)
    flat_far = far.T.reshape(-1)
    total = flat_group.shape[0]
    far_place = count(
        (flat_group[None, :] == flat_group[:, None]) & flat_far[None, :] & earlier(total)
    ).reshape(groups, sources).T
    return dict(
        source_row=source_row,
        to_group=to_group,
        to_within=to_within,
        order=order,
        kind=kind,
        far=far,
        far_round=far_round,
        far_place=far_place,
        rounds=rounds,
    )


def unwritten(shape, dtype):
    return pl.pallas_call(
        lambda out: None,
        out_shape=jax.ShapeDtypeStruct(shape, dtype),
        out_specs=pl.BlockSpec(memory_space=pl.ANY),
    )()


def update_kernel(parts, scalars, *refs):
    left = refs[:parts]
    right = refs[parts]
    old = refs[parts + 1 : 2 * parts + 1]
    out = refs[2 * parts + 1]
    lhs = jnp.concatenate([part[0] for part in left], axis=0)
    change = lax.dot_general(
        lhs, right[...], (((1,), (1,)), ((), ())), preferred_element_type=jnp.float32
    )
    for part in range(parts):
        new = old[part][...].astype(jnp.float32) - change[part * TILE : (part + 1) * TILE]
        out[part] = new.astype(out.dtype)


def update_chunk(mine, theirs, first, contrib, scalars, chunk, width, groups):
    parts = 4 if groups % 4 == 0 else 1
    depth = mine.shape[1]
    block = min(width, 1024)
    steps = width // block
    tiles = mine.reshape(-1, TILE, depth)
    left_specs = [
        pl.BlockSpec((1, TILE, depth), lambda n, m, s, part=part: (s[m * parts + part], 0, 0))
        for part in range(parts)
    ]
    right_spec = pl.BlockSpec((block, depth), lambda n, m, s: (first // block + n, 0))
    old_specs = [
        pl.BlockSpec(
            (TILE, block),
            lambda n, m, s, part=part: (s[m * parts + part], s[groups + chunk] // block + n),
        )
        for part in range(parts)
    ]
    return pl.pallas_call(
        lambda *refs: update_kernel(parts, *refs),
        out_shape=jax.ShapeDtypeStruct((groups, TILE, width), contrib.dtype),
        grid_spec=pltpu.PrefetchScalarGridSpec(
            num_scalar_prefetch=1,
            grid=(steps, groups // parts),
            in_specs=left_specs + [right_spec] + old_specs,
            out_specs=pl.BlockSpec((parts, TILE, block), lambda n, m, s: (m, 0, n)),
        ),
        name="update",
    )(scalars, *([tiles] * parts), theirs, *([contrib] * parts))


def assemble(row_code, row_from, starts, col_code, has_cross, recv, near, far, cross_recv, cross_near, init, block):
    fronts, per_rows = row_code.shape
    per_cols = col_code.shape[1]
    chunks = len(recv)
    moves_of = [recv] + near
    cross_of = [cross_recv] + cross_near
    sources = len(moves_of)
    widths = [part.shape[2] for part in recv]
    offsets = [sum(widths[:chunk]) for chunk in range(chunks)]
    span = sum(widths)
    cross_span = cross_recv.shape[2]
    vectors = block.shape[1]
    cap = recv[0].shape[0]
    scalars = jnp.concatenate(
        [
            row_code.reshape(-1),
            col_code.reshape(-1),
            has_cross.astype(jnp.int32).reshape(1),
            row_from.reshape(-1),
            starts.reshape(-1),
        ]
    ).astype(jnp.int32)
    col_base = fronts * per_rows
    flag = col_base + fronts * per_cols
    from_base = flag + 1
    start_base = from_base + fronts * per_rows

    def kernel(s, *refs):
        main_refs = [refs[k * chunks : (k + 1) * chunks] for k in range(sources)]
        refs = refs[sources * chunks :]
        cross_refs, refs = refs[:sources], refs[sources:]
        far_ref, init_ref, block_ref, schur_ref, product_ref, held, rounded, sems = refs
        step = pl.program_id(0)

        def moves(b, act):
            slot = b % 2
            for f in range(fronts):
                code = s[f * per_rows + b]
                index = code % cap
                source_row = s[from_base + f * per_rows + b]
                places = [
                    pl.multiple_of(s[start_base + source_row * chunks + chunk], TILE)
                    for chunk in range(chunks)
                ]

                def go(source, place, lanes, which, offset=None):
                    act(
                        pltpu.make_async_copy(
                            source.at[index]
                            if offset is None
                            else source.at[index, :, pl.ds(offset, lanes)],
                            held.at[slot, f, :, pl.ds(place, lanes)],
                            sems.at[slot, f, which],
                        )
                    )

                for k in range(sources):

                    @pl.when((code >= k * cap) & (code < (k + 1) * cap))
                    def _(k=k):
                        for chunk in range(chunks):
                            go(main_refs[k][chunk], places[chunk], widths[chunk], chunk)

                        @pl.when(s[flag] > 0)
                        def _():
                            go(cross_refs[k], span, cross_span, chunks)

                @pl.when(code >= sources * cap)
                def _():
                    for chunk in range(chunks):
                        go(far_ref, places[chunk], widths[chunk], chunk, offsets[chunk])

                    @pl.when(s[flag] > 0)
                    def _():
                        go(far_ref, span, cross_span, chunks, span)

        @pl.when(step == 0)
        def _():
            moves(step, lambda copy: copy.start())

        @pl.when(step + 1 < per_rows)
        def _():
            moves(step + 1, lambda copy: copy.start())

        moves(step, lambda copy: copy.wait())
        slot = step % 2

        def column(c, carry):
            lanes = pl.ds(pl.multiple_of(c * TILE, TILE), TILE)
            total = init_ref[:, lanes].astype(jnp.float32)
            for f in range(fronts):
                code = s[col_base + f * per_cols + c]
                used = (code >= 0) & (s[f * per_rows + step] >= 0)
                place = pl.multiple_of(jnp.maximum(code, 0) * TILE, TILE)
                piece = held[slot, f, :, pl.ds(place, TILE)].astype(jnp.float32)
                total = total + jnp.where(used, piece, 0.0)
            schur_ref[:, lanes] = total
            rounded[:, lanes] = total.astype(jnp.bfloat16)
            return carry

        lax.fori_loop(0, per_cols, column, 0, unroll=2)
        product_ref[...] = jnp.dot(
            rounded[...], block_ref[...], preferred_element_type=jnp.float32
        )

    anywhere = pl.BlockSpec(memory_space=pl.ANY)
    wide = per_cols * TILE
    return pl.pallas_call(
        kernel,
        out_shape=(
            jax.ShapeDtypeStruct((per_rows * TILE, wide), jnp.float32),
            jax.ShapeDtypeStruct((per_rows * TILE, vectors), jnp.float32),
        ),
        grid_spec=pltpu.PrefetchScalarGridSpec(
            num_scalar_prefetch=1,
            grid=(per_rows,),
            in_specs=[anywhere] * (sources * (chunks + 1) + 1)
            + [
                pl.BlockSpec((TILE, wide), lambda b, s: (b, 0)),
                pl.BlockSpec((wide, vectors), lambda b, s: (0, 0)),
            ],
            out_specs=[
                pl.BlockSpec((TILE, wide), lambda b, s: (b, 0)),
                pl.BlockSpec((TILE, vectors), lambda b, s: (b, 0)),
            ],
            scratch_shapes=[
                pltpu.VMEM((2, fronts, TILE, span + cross_span), jnp.bfloat16),
                pltpu.VMEM((TILE, wide), jnp.bfloat16),
                pltpu.SemaphoreType.DMA((2, fronts, chunks + 1)),
            ],
        ),
        name="assemble",
    )(scalars, *[part for parts in moves_of for part in parts], *cross_of, far, init, block)


def shards(pivot_block, border, contrib, inverses, row_tiles, col_tiles, owner, schur_init, block):
    n_front = lax.axis_size("front")
    n_row = lax.axis_size("row")
    n_col = lax.axis_size("col")
    front_index = lax.axis_index("front")
    row_index = lax.axis_index("row")
    col_index = lax.axis_index("col")
    groups = n_front * n_row
    slots_all = owner.shape[0]
    row_span = border.shape[1]
    col_span = contrib.shape[2]
    tile_rows = row_span // TILE
    tile_cols = col_span // TILE
    rows_per_group = slots_all // groups
    cols_per_group = slots_all // n_col
    by_hops = takes_hops(n_row, n_col) and col_span == 2 * row_span
    me = front_index * n_row + row_index

    lower = pivot_panels(pivot_block[0], inverses[0])
    mine = eliminate(border[0], inverses[0], lower)
    if by_hops:
        first, second, others = collect_border(border[0], row_index, col_index)
        half = row_span // 2
        widths = [half // 2, half // 2, half, half, half // 2, half // 2]
        lines = jnp.arange(n_row)
        turned = jnp.where(col_index == 0, lines > 0, lines == n_row - 1).astype(jnp.int32)
        mine_half = half * (2 * turned + col_index)
        starts = jnp.stack(
            [
                mine_half,
                mine_half + half // 2,
                half * (2 * turned + 1 - col_index),
                half * (2 - 2 * turned + col_index),
                half * (3 - 2 * turned - col_index),
                half * (3 - 2 * turned - col_index) + half // 2,
            ],
            axis=1,
        )
    else:
        share = row_span // n_col
        own_rows = lax.dynamic_slice_in_dim(mine, col_index * share, share, 0)
        factor = lax.all_gather(own_rows, ("row", "col"), axis=0, tiled=True)
        whole = lax.dynamic_slice_in_dim(factor, col_index * col_span, col_span, 0)
        widths = [col_span // CHUNKS] * CHUNKS
        starts = jnp.broadcast_to(jnp.arange(CHUNKS) * widths[0], (n_row, CHUNKS))
    chunks = len(widths)
    my_starts = lax.dynamic_index_in_dim(starts, row_index, 0, keepdims=False)

    slot_rows = owner[row_tiles].reshape(groups, tile_rows)
    kinds = [(1, ROW_CAP)] + [
        (n_row * other, FRONT_CAPS[(other - 1) % len(FRONT_CAPS)]) for other in range(1, n_front)
    ]
    plan = row_plan(slot_rows, rows_per_group, groups, kinds)
    held = lambda table: lax.dynamic_index_in_dim(table, me, 1, keepdims=False)
    my_group = held(plan["to_group"])
    my_order = held(plan["order"])
    my_kind = held(plan["kind"])
    near_index = [
        jnp.sum(
            (
                (my_kind == index + 1)[None, :] & (my_order[None, :] == jnp.arange(room)[:, None])
            ).astype(jnp.int32)
            * jnp.arange(groups),
            axis=-1,
        )
        for index, (_, room) in enumerate(kinds)
    ]
    for_me = plan["to_group"] == me
    code = groups * plan["kind"] + jnp.where(
        plan["kind"] == 0,
        jnp.arange(groups)[:, None],
        jnp.where(plan["far"], plan["far_place"], plan["order"]),
    )
    hit = for_me[:, :, None] & (plan["to_within"][:, :, None] == jnp.arange(rows_per_group))
    row_code = (
        jnp.sum(
            jnp.where(hit, code[:, :, None] + 1, 0).reshape(
                n_front, n_row * groups, rows_per_group
            ),
            axis=1,
        )
        - 1
    )

    row_from = jnp.sum(
        jnp.where(hit, (jnp.arange(groups) % n_row)[:, None, None], 0).reshape(
            n_front, n_row * groups, rows_per_group
        ),
        axis=1,
    )

    slot_cols = owner[col_tiles].reshape(n_front, n_col, tile_cols)
    to_col = slot_cols // cols_per_group
    within_col = slot_cols % cols_per_group
    crossing = to_col != jnp.arange(n_col)[None, :, None]
    cross_order = count(
        (to_col[..., :, None] == to_col[..., None, :]) & earlier(tile_cols)[None, None]
    )
    cross_rounds = jnp.max(jnp.where(crossing, cross_order + 1, 0))
    flat_to = to_col.reshape(n_front, -1)
    flat_cross = crossing.reshape(n_front, -1)
    cross_place = count(
        (flat_to[:, :, None] == flat_to[:, None, :])
        & flat_cross[:, None, :]
        & earlier(n_col * tile_cols)[None]
    ).reshape(n_front, n_col, tile_cols)
    col_place = jnp.where(crossing, tile_cols + cross_place, jnp.arange(tile_cols))
    col_hit = (to_col == col_index)[..., None] & (
        within_col[..., None] == jnp.arange(cols_per_group)
    )
    col_code = jnp.sum(jnp.where(col_hit, col_place[..., None] + 1, 0), axis=(1, 2)) - 1
    my_to = to_col[front_index]
    my_cross_order = cross_order[front_index]
    my_cross_place = cross_place[front_index]

    scalars = jnp.concatenate(
        [
            lax.dynamic_index_in_dim(plan["source_row"], me, 0, keepdims=False),
            my_starts,
        ]
    ).astype(jnp.int32)

    def across(rows, step):
        return lax.ppermute(rows, FR, [(g, g ^ step) for g in range(groups)])

    def settle(received):
        picked, moved = [], []
        for index, (step, _) in enumerate(kinds):
            picked.append(jnp.take(received, near_index[index], axis=0, mode="clip"))
            moved.append(across(picked[-1], step))
        return picked, moved

    sent, recv, near, picks = [], [], [], []
    for chunk in range(chunks):
        offset = 0
        if not by_hops:
            theirs, offset = whole, chunk * widths[0]
        elif chunk < 2:
            theirs = eliminate(first(chunk, sent[-1] if sent else None), inverses[0], lower)
        elif chunk == 2:
            theirs = eliminate(second(sent[-1]), inverses[0], lower)
            later = [eliminate(part, inverses[0], lower) for part in others(theirs)]
        elif chunk == 3:
            theirs = later[0]
        else:
            theirs, offset = later[1], (chunk - 4) * widths[chunk]
        width = widths[chunk]
        piece = update_chunk(mine, theirs, offset, contrib[0], scalars, chunk, width, groups)
        if chunk >= 2:
            piece, picks[chunk - 2] = lax.optimization_barrier((piece, picks[chunk - 2]))
        sent.append(piece)
        recv.append(lax.all_to_all(piece, FR, split_axis=0, concat_axis=0, tiled=True))
        picked, moved = settle(recv[chunk])
        picks.append(picked)
        near.append(moved)

    near = [[moved[index] for moved in near] for index in range(len(kinds))]

    cross_span = (tile_cols + 1) * TILE

    def cross_round(state):
        turn, buffer = state
        picks = []
        for other in range(n_col):
            chosen = (my_to[col_index] == other) & (my_cross_order[col_index] == turn)
            column = jnp.sum(chosen.astype(jnp.int32) * jnp.arange(tile_cols))
            pick = None
            for chunk in range(chunks):
                local = column - my_starts[chunk] // TILE
                most = widths[chunk] // TILE - 1
                inside = (local >= 0) & (local <= most)
                part = lax.dynamic_slice_in_dim(
                    sent[chunk], jnp.clip(local, 0, most) * TILE, TILE, 2
                )
                pick = part if pick is None else jnp.where(inside, part, pick)
            picks.append(pick)
        arrived = lax.all_to_all(jnp.stack(picks), "col", split_axis=0, concat_axis=0, tiled=True)
        for other in range(n_col):
            chosen = (
                (my_to[other] == col_index) & (my_cross_order[other] == turn) & (other != col_index)
            )
            place = jnp.where(
                jnp.any(chosen),
                jnp.sum(jnp.where(chosen, my_cross_place[other], 0)),
                tile_cols,
            )
            buffer = lax.dynamic_update_slice_in_dim(buffer, arrived[other], place * TILE, 2)
        return (turn + 1, buffer)

    cross_rounds, _ = lax.optimization_barrier((cross_rounds, recv[-1]))
    far_rounds, _ = lax.optimization_barrier((jnp.cumsum(plan["rounds"]), recv[-1]))
    crossed = unwritten((groups, TILE, cross_span), contrib.dtype)
    _, crossed = lax.while_loop(
        lambda state: state[0] < cross_rounds, cross_round, (jnp.int32(0), crossed)
    )

    def cross_exchange(state):
        mark = jnp.full((1, 1, TILE), state[0], contrib.dtype)
        outgoing = lax.dynamic_update_slice(state[1], mark, (0, 0, tile_cols * TILE))
        received = lax.all_to_all(outgoing, FR, split_axis=0, concat_axis=0, tiled=True)
        return (cross_rounds, outgoing, received, settle(received)[1])

    _, _, cross_recv, cross_near = lax.while_loop(
        lambda state: state[0] < cross_rounds,
        cross_exchange,
        (
            jnp.int32(0),
            crossed,
            unwritten((groups, TILE, cross_span), contrib.dtype),
            [unwritten((room, TILE, cross_span), contrib.dtype) for _, room in kinds],
        ),
    )

    my_far = held(plan["far"])
    my_far_round = held(plan["far_round"])

    def far_exchange(state):
        turn, buffer = state
        step = count(far_rounds <= turn)
        turn_of = turn - jnp.where(step > 0, far_rounds[jnp.maximum(step - 1, 0)], 0)
        chosen = my_far & (my_far_round == turn_of) & (my_group == (me ^ step))
        index = jnp.sum(chosen.astype(jnp.int32) * jnp.arange(groups))
        row = jnp.concatenate(
            [
                lax.dynamic_slice_in_dim(part, index, 1, 0)
                for part in recv + [cross_recv]
            ],
            axis=2,
        )
        arrived = lax.switch(
            step - 1,
            [lambda row, step=step: across(row, step) for step in range(1, groups)],
            row,
        )
        coming = (
            plan["far"]
            & for_me
            & (plan["far_round"] == turn_of)
            & (jnp.arange(groups)[None, :] == (me ^ step))
        )
        place = jnp.where(
            jnp.any(coming), jnp.sum(jnp.where(coming, plan["far_place"], 0)), groups
        )
        return (turn + 1, lax.dynamic_update_slice_in_dim(buffer, arrived, place, 0))

    far = unwritten((groups + 1, TILE, col_span + cross_span), contrib.dtype)
    _, far = lax.while_loop(
        lambda state: state[0] < far_rounds[-1], far_exchange, (jnp.int32(0), far)
    )

    schur, partial = assemble(
        row_code,
        row_from,
        starts,
        col_code,
        cross_rounds > 0,
        recv,
        near,
        far,
        cross_recv,
        cross_near,
        schur_init,
        block,
    )
    if n_col == 2:
        part = partial.shape[0] // n_col
        keep = lax.dynamic_slice_in_dim(partial, col_index * part, part, 0)
        give = lax.dynamic_slice_in_dim(partial, (1 - col_index) * part, part, 0)
        product = keep + lax.ppermute(give, "col", [(0, 1), (1, 0)])
    else:
        product = lax.psum_scatter(partial, "col", scatter_dimension=0, tiled=True)
    return (schur, product)


def takes_hops(n_row, n_col):
    return n_row == 4 and n_col == 2


def solution(mesh):
    in_specs = (
        P("front", None, None),
        P("front", "row", None),
        P("front", "row", "col"),
        P("front", None, None, None),
        P(),
        P(),
        P(),
        P(("front", "row"), "col"),
        P("col", None),
    )
    out_specs = (P(("front", "row"), "col"), P(("front", "row", "col"), None))

    return jax.shard_map(shards, mesh=mesh, in_specs=in_specs, out_specs=out_specs, check_vma=False)
```

```python
import jax
import jax.numpy as jnp
from jax import lax
from jax.experimental import pallas as pl
from jax.experimental.pallas import tpu as pltpu
from jax.sharding import PartitionSpec as P


TILE = 128
CHUNKS = 4
ROW_CAP = 6
FRONT_CAPS = (6, 4, 3)
FR = ("front", "row")


def pivot_kernel(pivot, inverse_set, out):
    panels, width, _ = inverse_set.shape
    now = {
        (i, j): pivot[i * width : (i + 1) * width, j * width : (j + 1) * width].astype(jnp.float32)
        for i in range(panels)
        for j in range(i + 1)
    }
    out[...] = jnp.zeros_like(out)
    for k in range(panels - 1):
        lower = {}
        for i in range(k + 1, panels):
            lower[i] = jnp.dot(
                now[i, k].astype(jnp.bfloat16), inverse_set[k], preferred_element_type=jnp.float32
            ).astype(jnp.bfloat16)
            out[k, i * width : (i + 1) * width, :] = lower[i]
        for i in range(k + 1, panels):
            for j in range(k + 1, i + 1):
                now[i, j] = now[i, j] - lax.dot_general(
                    lower[i], lower[j], (((1,), (1,)), ((), ())), preferred_element_type=jnp.float32
                )


def pivot_panels(pivot, inverse_set):
    panels, width, _ = inverse_set.shape
    return pl.pallas_call(
        pivot_kernel,
        out_shape=jax.ShapeDtypeStruct((panels, pivot.shape[0], width), jnp.bfloat16),
        name="pivot",
    )(pivot, inverse_set)


def rows_kernel(rows, inverse_set, lower, out):
    panels, width, _ = inverse_set.shape
    now = [rows[:, j * width : (j + 1) * width].astype(jnp.float32) for j in range(panels)]
    for k in range(panels):
        side = jnp.dot(
            now[k].astype(jnp.bfloat16), inverse_set[k], preferred_element_type=jnp.float32
        ).astype(jnp.bfloat16)
        out[:, k * width : (k + 1) * width] = side
        for j in range(k + 1, panels):
            now[j] = now[j] - lax.dot_general(
                side,
                lower[k, j * width : (j + 1) * width, :],
                (((1,), (1,)), ((), ())),
                preferred_element_type=jnp.float32,
            )


def eliminate(rows, inverse_set, lower):
    size, depth = rows.shape
    step = min(size, 256)
    return pl.pallas_call(
        rows_kernel,
        out_shape=jax.ShapeDtypeStruct(rows.shape, jnp.bfloat16),
        grid=(size // step,),
        in_specs=[
            pl.BlockSpec((step, depth), lambda i: (i, 0)),
            pl.BlockSpec(inverse_set.shape, lambda i: (0, 0, 0)),
            pl.BlockSpec(lower.shape, lambda i: (0, 0, 0)),
        ],
        out_specs=pl.BlockSpec((step, depth), lambda i: (i, 0)),
        name="eliminate",
    )(rows, inverse_set, lower)


def collect_border(own, row_index, col_index):
    n_row = 4
    half = own.shape[0] // 2
    part = half // 2
    up = [(z, z + 1) for z in range(n_row - 1)]
    down = [(z + 1, z) for z in range(n_row - 1)]
    first_row = col_index * half
    pieces = [lax.dynamic_slice_in_dim(own, first_row + p * part, part, 0) for p in range(2)]
    rest = lax.dynamic_slice_in_dim(own, half - first_row, half, 0)
    held = (row_index // 2) == col_index
    left = col_index == 0

    def by_row(options):
        chosen = options[0]
        for z in range(1, n_row):
            chosen = jnp.where(row_index == z, options[z], chosen)
        return chosen

    below = [[piece] for piece in pieces]
    above = [[piece] for piece in pieces]
    for p in range(2):
        for _ in range(n_row - 1):
            below[p].append(lax.ppermute(below[p][-1], "row", up))
            above[p].append(lax.ppermute(above[p][-1], "row", down))
    swapped = [None, None]

    def first(p, done):
        options = [above[p][2], above[p][1], below[p][1], below[p][2]]
        if done is not None:
            _, options = lax.optimization_barrier((done, options))
        near = by_row(options)
        swapped[p] = lax.ppermute(near, ("row", "col"), [(0, 1), (2, 3), (5, 4), (7, 6)])
        return jnp.where(held, pieces[p], near)

    def second(done):
        _, arrived = lax.optimization_barrier((done, swapped))
        return jnp.where(held, rest, jnp.concatenate(arrived))

    def others(done):
        _, ups, downs = lax.optimization_barrier((done, below, above))
        low = [by_row([d[1], u[1], u[2], u[3]]) for u, d in zip(ups, downs)]
        high = [by_row([d[3], d[2], d[1], u[1]]) for u, d in zip(ups, downs)]
        keep = jnp.concatenate([jnp.where(left, a, b) for a, b in zip(low, high)])
        give = jnp.concatenate([jnp.where(left, b, a) for a, b in zip(low, high)])
        other = lax.ppermute(give, "col", [(0, 1), (1, 0)])
        return keep, other

    return first, second, others


def count(mask, axis=-1):
    return jnp.sum(mask.astype(jnp.int32), axis=axis)


def earlier(n):
    return jnp.arange(n)[None, :] < jnp.arange(n)[:, None]


def row_plan(slot_rows, per_group, groups, kinds):
    sources, tile_rows = slot_rows.shape
    places = jnp.arange(groups)
    target = slot_rows // per_group
    within = slot_rows % per_group
    same = target[:, :, None] == target[:, None, :]
    extra = count(same & earlier(tile_rows)[None]) > 0
    amount = count(target[:, None, :] == places[None, :, None])
    double = amount > 1
    empty = amount == 0
    landing = jnp.zeros_like(amount)
    for step, _ in kinds[1:]:
        match = double & empty[:, places ^ step]
        landing = jnp.where(match, places ^ step, landing)
        double = double & ~match
        empty = empty & ~match[:, places ^ step]
    double_order = count(double[:, None, :] & earlier(groups)[None])
    empty_order = count(empty[:, None, :] & earlier(groups)[None])
    left = (
        double[:, :, None]
        & empty[:, None, :]
        & (double_order[:, :, None] == empty_order[:, None, :])
    )
    landing = landing + jnp.sum(left.astype(jnp.int32) * places, axis=-1)
    extra_place = jnp.sum(
        (target[:, :, None] == places).astype(jnp.int32) * landing[:, None, :], axis=-1
    )
    lands = (
        jnp.where(extra, extra_place, target)[:, None, :] == places[None, :, None]
    ).astype(jnp.int32)
    source_row = jnp.sum(lands * jnp.arange(tile_rows), axis=-1)
    to_group = jnp.sum(lands * target[:, None, :], axis=-1)
    to_within = jnp.sum(lands * within[:, None, :], axis=-1)
    here = places[None, :]
    astray = to_group != here
    order = count(
        (to_group[:, None, :] == to_group[None, :, :])
        & astray[None]
        & earlier(sources)[:, :, None],
        axis=1,
    )
    steps = to_group ^ here
    kind = jnp.zeros_like(order)
    far_round = order
    for index, (step, room) in enumerate(kinds):
        kind = jnp.where(astray & (steps == step) & (order < room), index + 1, kind)
        far_round = jnp.where(steps == step, order - room, far_round)
    far = astray & (kind == 0)
    kind = jnp.where(far, len(kinds) + 1, kind)
    rounds = jnp.max(
        jnp.where(far & (steps == places[:, None, None]), far_round + 1, 0), axis=(1, 2)
    )
    flat_group = to_group.T.reshape(-1)
    flat_far = far.T.reshape(-1)
    total = flat_group.shape[0]
    far_place = count(
        (flat_group[None, :] == flat_group[:, None]) & flat_far[None, :] & earlier(total)
    ).reshape(groups, sources).T
    return dict(
        source_row=source_row,
        to_group=to_group,
        to_within=to_within,
        order=order,
        kind=kind,
        far=far,
        far_round=far_round,
        far_place=far_place,
        rounds=rounds,
    )


def unwritten(shape, dtype):
    return pl.pallas_call(
        lambda out: None,
        out_shape=jax.ShapeDtypeStruct(shape, dtype),
        out_specs=pl.BlockSpec(memory_space=pl.ANY),
    )()


def update_kernel(parts, scalars, *refs):
    left = refs[:parts]
    right = refs[parts]
    old = refs[parts + 1 : 2 * parts + 1]
    out = refs[2 * parts + 1]
    lhs = jnp.concatenate([part[0] for part in left], axis=0)
    change = lax.dot_general(
        lhs, right[...], (((1,), (1,)), ((), ())), preferred_element_type=jnp.float32
    )
    for part in range(parts):
        new = old[part][...].astype(jnp.float32) - change[part * TILE : (part + 1) * TILE]
        out[part] = new.astype(out.dtype)


def update_chunk(mine, theirs, first, contrib, scalars, chunk, width, groups):
    parts = 2
    depth = mine.shape[1]
    block = min(width, 512)
    steps = width // block
    tiles = mine.reshape(-1, TILE, depth)
    left_specs = [
        pl.BlockSpec((1, TILE, depth), lambda n, m, s, part=part: (s[m * parts + part], 0, 0))
        for part in range(parts)
    ]
    right_spec = pl.BlockSpec((block, depth), lambda n, m, s: (first // block + n, 0))
    old_specs = [
        pl.BlockSpec(
            (TILE, block),
            lambda n, m, s, part=part: (s[m * parts + part], s[groups + chunk] // block + n),
        )
        for part in range(parts)
    ]
    return pl.pallas_call(
        lambda *refs: update_kernel(parts, *refs),
        out_shape=jax.ShapeDtypeStruct((groups, TILE, width), contrib.dtype),
        grid_spec=pltpu.PrefetchScalarGridSpec(
            num_scalar_prefetch=1,
            grid=(steps, groups // parts),
            in_specs=left_specs + [right_spec] + old_specs,
            out_specs=pl.BlockSpec((parts, TILE, block), lambda n, m, s: (m, 0, n)),
        ),
        name="update",
    )(scalars, *([tiles] * parts), theirs, *([contrib] * parts))


def assemble(row_code, row_from, starts, col_code, has_cross, recv, near, far, cross_recv, cross_near, init, block):
    fronts, per_rows = row_code.shape
    per_cols = col_code.shape[1]
    chunks = len(recv)
    moves_of = [recv] + near
    cross_of = [cross_recv] + cross_near
    sources = len(moves_of)
    widths = [part.shape[2] for part in recv]
    offsets = [sum(widths[:chunk]) for chunk in range(chunks)]
    span = sum(widths)
    cross_span = cross_recv.shape[2]
    vectors = block.shape[1]
    cap = recv[0].shape[0]
    scalars = jnp.concatenate(
        [
            row_code.reshape(-1),
            col_code.reshape(-1),
            has_cross.astype(jnp.int32).reshape(1),
            row_from.reshape(-1),
            starts.reshape(-1),
        ]
    ).astype(jnp.int32)
    col_base = fronts * per_rows
    flag = col_base + fronts * per_cols
    from_base = flag + 1
    start_base = from_base + fronts * per_rows

    def kernel(s, *refs):
        main_refs = [refs[k * chunks : (k + 1) * chunks] for k in range(sources)]
        refs = refs[sources * chunks :]
        cross_refs, refs = refs[:sources], refs[sources:]
        far_ref, init_ref, block_ref, schur_ref, product_ref, held, rounded, sems = refs
        step = pl.program_id(0)

        def moves(b, act):
            slot = b % 2

            @pl.loop(0, fronts)
            def _(f):
                code = s[f * per_rows + b]
                index = code % cap
                source_row = s[from_base + f * per_rows + b]
                places = [
                    pl.multiple_of(s[start_base + source_row * chunks + chunk], TILE)
                    for chunk in range(chunks)
                ]

                def go(source, place, lanes, which, offset=None):
                    act(
                        pltpu.make_async_copy(
                            source.at[index]
                            if offset is None
                            else source.at[index, :, pl.ds(offset, lanes)],
                            held.at[slot, f, :, pl.ds(place, lanes)],
                            sems.at[slot, f, which],
                        )
                    )

                for k in range(sources):

                    @pl.when((code >= k * cap) & (code < (k + 1) * cap))
                    def _(k=k):
                        for chunk in range(chunks):
                            go(main_refs[k][chunk], places[chunk], widths[chunk], chunk)

                        @pl.when(s[flag] > 0)
                        def _():
                            go(cross_refs[k], span, cross_span, chunks)

                @pl.when(code >= sources * cap)
                def _():
                    for chunk in range(chunks):
                        go(far_ref, places[chunk], widths[chunk], chunk, offsets[chunk])

                    @pl.when(s[flag] > 0)
                    def _():
                        go(far_ref, span, cross_span, chunks, span)

        @pl.when(step == 0)
        def _():
            moves(step, lambda copy: copy.start())

        @pl.when(step + 1 < per_rows)
        def _():
            moves(step + 1, lambda copy: copy.start())

        moves(step, lambda copy: copy.wait())
        slot = step % 2

        def column(c, carry):
            lanes = pl.ds(pl.multiple_of(c * TILE, TILE), TILE)
            total = init_ref[:, lanes].astype(jnp.float32)
            for f in range(fronts):
                code = s[col_base + f * per_cols + c]
                used = (code >= 0) & (s[f * per_rows + step] >= 0)
                place = pl.multiple_of(jnp.maximum(code, 0) * TILE, TILE)
                piece = held[slot, f, :, pl.ds(place, TILE)].astype(jnp.float32)
                total = total + jnp.where(used, piece, 0.0)
            schur_ref[:, lanes] = total
            rounded[:, lanes] = total.astype(jnp.bfloat16)
            return carry

        lax.fori_loop(0, per_cols, column, 0, unroll=2)
        product_ref[...] = jnp.dot(
            rounded[...], block_ref[...], preferred_element_type=jnp.float32
        )

    anywhere = pl.BlockSpec(memory_space=pl.ANY)
    wide = per_cols * TILE
    return pl.pallas_call(
        kernel,
        out_shape=(
            jax.ShapeDtypeStruct((per_rows * TILE, wide), jnp.float32),
            jax.ShapeDtypeStruct((per_rows * TILE, vectors), jnp.float32),
        ),
        grid_spec=pltpu.PrefetchScalarGridSpec(
            num_scalar_prefetch=1,
            grid=(per_rows,),
            in_specs=[anywhere] * (sources * (chunks + 1) + 1)
            + [
                pl.BlockSpec((TILE, wide), lambda b, s: (b, 0)),
                pl.BlockSpec((wide, vectors), lambda b, s: (0, 0)),
            ],
            out_specs=[
                pl.BlockSpec((TILE, wide), lambda b, s: (b, 0)),
                pl.BlockSpec((TILE, vectors), lambda b, s: (b, 0)),
            ],
            scratch_shapes=[
                pltpu.VMEM((2, fronts, TILE, span + cross_span), jnp.bfloat16),
                pltpu.VMEM((TILE, wide), jnp.bfloat16),
                pltpu.SemaphoreType.DMA((2, fronts, chunks + 1)),
            ],
        ),
        name="assemble",
    )(scalars, *[part for parts in moves_of for part in parts], *cross_of, far, init, block)


def shards(pivot_block, border, contrib, inverses, row_tiles, col_tiles, owner, schur_init, block):
    n_front = lax.axis_size("front")
    n_row = lax.axis_size("row")
    n_col = lax.axis_size("col")
    front_index = lax.axis_index("front")
    row_index = lax.axis_index("row")
    col_index = lax.axis_index("col")
    groups = n_front * n_row
    slots_all = owner.shape[0]
    row_span = border.shape[1]
    col_span = contrib.shape[2]
    tile_rows = row_span // TILE
    tile_cols = col_span // TILE
    rows_per_group = slots_all // groups
    cols_per_group = slots_all // n_col
    by_hops = takes_hops(n_row, n_col) and col_span == 2 * row_span
    me = front_index * n_row + row_index

    lower = pivot_panels(pivot_block[0], inverses[0])
    mine = eliminate(border[0], inverses[0], lower)
    if by_hops:
        first, second, others = collect_border(border[0], row_index, col_index)
        half = row_span // 2
        widths = [half // 2, half // 2, half, half, half // 2, half // 2]
        lines = jnp.arange(n_row)
        turned = jnp.where(col_index == 0, lines > 0, lines == n_row - 1).astype(jnp.int32)
        mine_half = half * (2 * turned + col_index)
        starts = jnp.stack(
            [
                mine_half,
                mine_half + half // 2,
                half * (2 * turned + 1 - col_index),
                half * (2 - 2 * turned + col_index),
                half * (3 - 2 * turned - col_index),
                half * (3 - 2 * turned - col_index) + half // 2,
            ],
            axis=1,
        )
    else:
        share = row_span // n_col
        own_rows = lax.dynamic_slice_in_dim(mine, col_index * share, share, 0)
        factor = lax.all_gather(own_rows, ("row", "col"), axis=0, tiled=True)
        whole = lax.dynamic_slice_in_dim(factor, col_index * col_span, col_span, 0)
        widths = [col_span // CHUNKS] * CHUNKS
        starts = jnp.broadcast_to(jnp.arange(CHUNKS) * widths[0], (n_row, CHUNKS))
    chunks = len(widths)
    my_starts = lax.dynamic_index_in_dim(starts, row_index, 0, keepdims=False)

    slot_rows = owner[row_tiles].reshape(groups, tile_rows)
    kinds = [(1, ROW_CAP)] + [
        (n_row * other, FRONT_CAPS[(other - 1) % len(FRONT_CAPS)]) for other in range(1, n_front)
    ]
    plan = row_plan(slot_rows, rows_per_group, groups, kinds)
    held = lambda table: lax.dynamic_index_in_dim(table, me, 1, keepdims=False)
    my_group = held(plan["to_group"])
    my_order = held(plan["order"])
    my_kind = held(plan["kind"])
    near_index = [
        jnp.sum(
            (
                (my_kind == index + 1)[None, :] & (my_order[None, :] == jnp.arange(room)[:, None])
            ).astype(jnp.int32)
            * jnp.arange(groups),
            axis=-1,
        )
        for index, (_, room) in enumerate(kinds)
    ]
    for_me = plan["to_group"] == me
    code = groups * plan["kind"] + jnp.where(
        plan["kind"] == 0,
        jnp.arange(groups)[:, None],
        jnp.where(plan["far"], plan["far_place"], plan["order"]),
    )
    hit = for_me[:, :, None] & (plan["to_within"][:, :, None] == jnp.arange(rows_per_group))
    row_code = (
        jnp.sum(
            jnp.where(hit, code[:, :, None] + 1, 0).reshape(
                n_front, n_row * groups, rows_per_group
            ),
            axis=1,
        )
        - 1
    )

    row_from = jnp.sum(
        jnp.where(hit, (jnp.arange(groups) % n_row)[:, None, None], 0).reshape(
            n_front, n_row * groups, rows_per_group
        ),
        axis=1,
    )

    slot_cols = owner[col_tiles].reshape(n_front, n_col, tile_cols)
    to_col = slot_cols // cols_per_group
    within_col = slot_cols % cols_per_group
    crossing = to_col != jnp.arange(n_col)[None, :, None]
    cross_order = count(
        (to_col[..., :, None] == to_col[..., None, :]) & earlier(tile_cols)[None, None]
    )
    cross_rounds = jnp.max(jnp.where(crossing, cross_order + 1, 0))
    flat_to = to_col.reshape(n_front, -1)
    flat_cross = crossing.reshape(n_front, -1)
    cross_place = count(
        (flat_to[:, :, None] == flat_to[:, None, :])
        & flat_cross[:, None, :]
        & earlier(n_col * tile_cols)[None]
    ).reshape(n_front, n_col, tile_cols)
    col_place = jnp.where(crossing, tile_cols + cross_place, jnp.arange(tile_cols))
    col_hit = (to_col == col_index)[..., None] & (
        within_col[..., None] == jnp.arange(cols_per_group)
    )
    col_code = jnp.sum(jnp.where(col_hit, col_place[..., None] + 1, 0), axis=(1, 2)) - 1
    my_to = to_col[front_index]
    my_cross_order = cross_order[front_index]
    my_cross_place = cross_place[front_index]

    scalars = jnp.concatenate(
        [
            lax.dynamic_index_in_dim(plan["source_row"], me, 0, keepdims=False),
            my_starts,
        ]
    ).astype(jnp.int32)

    def across(rows, step):
        return lax.ppermute(rows, FR, [(g, g ^ step) for g in range(groups)])

    def settle(received):
        picked, moved = [], []
        for index, (step, _) in enumerate(kinds):
            picked.append(jnp.take(received, near_index[index], axis=0, mode="clip"))
            moved.append(across(picked[-1], step))
        return picked, moved

    sent, recv, near, picks = [], [], [], []
    for chunk in range(chunks):
        offset = 0
        if not by_hops:
            theirs, offset = whole, chunk * widths[0]
        elif chunk < 2:
            theirs = eliminate(first(chunk, sent[-1] if sent else None), inverses[0], lower)
        elif chunk == 2:
            theirs = eliminate(second(sent[-1]), inverses[0], lower)
            later = [eliminate(part, inverses[0], lower) for part in others(theirs)]
        elif chunk == 3:
            theirs = later[0]
        else:
            theirs, offset = later[1], (chunk - 4) * widths[chunk]
        width = widths[chunk]
        piece = update_chunk(mine, theirs, offset, contrib[0], scalars, chunk, width, groups)
        if chunk >= 2:
            piece, picks[chunk - 2] = lax.optimization_barrier((piece, picks[chunk - 2]))
        sent.append(piece)
        recv.append(lax.all_to_all(piece, FR, split_axis=0, concat_axis=0, tiled=True))
        picked, moved = settle(recv[chunk])
        picks.append(picked)
        near.append(moved)

    near = [[moved[index] for moved in near] for index in range(len(kinds))]

    cross_span = (tile_cols + 1) * TILE

    def cross_round(state):
        turn, buffer = state
        picks = []
        for other in range(n_col):
            chosen = (my_to[col_index] == other) & (my_cross_order[col_index] == turn)
            column = jnp.sum(chosen.astype(jnp.int32) * jnp.arange(tile_cols))
            pick = None
            for chunk in range(chunks):
                local = column - my_starts[chunk] // TILE
                most = widths[chunk] // TILE - 1
                inside = (local >= 0) & (local <= most)
                part = lax.dynamic_slice_in_dim(
                    sent[chunk], jnp.clip(local, 0, most) * TILE, TILE, 2
                )
                pick = part if pick is None else jnp.where(inside, part, pick)
            picks.append(pick)
        arrived = lax.all_to_all(jnp.stack(picks), "col", split_axis=0, concat_axis=0, tiled=True)
        for other in range(n_col):
            chosen = (
                (my_to[other] == col_index) & (my_cross_order[other] == turn) & (other != col_index)
            )
            place = jnp.where(
                jnp.any(chosen),
                jnp.sum(jnp.where(chosen, my_cross_place[other], 0)),
                tile_cols,
            )
            buffer = lax.dynamic_update_slice_in_dim(buffer, arrived[other], place * TILE, 2)
        return (turn + 1, buffer)

    cross_rounds, _ = lax.optimization_barrier((cross_rounds, recv[-1]))
    far_rounds, _ = lax.optimization_barrier((jnp.cumsum(plan["rounds"]), recv[-1]))
    crossed = unwritten((groups, TILE, cross_span), contrib.dtype)
    _, crossed = lax.while_loop(
        lambda state: state[0] < cross_rounds, cross_round, (jnp.int32(0), crossed)
    )

    def cross_exchange(state):
        mark = jnp.full((1, 1, TILE), state[0], contrib.dtype)
        outgoing = lax.dynamic_update_slice(state[1], mark, (0, 0, tile_cols * TILE))
        received = lax.all_to_all(outgoing, FR, split_axis=0, concat_axis=0, tiled=True)
        return (cross_rounds, outgoing, received, settle(received)[1])

    _, _, cross_recv, cross_near = lax.while_loop(
        lambda state: state[0] < cross_rounds,
        cross_exchange,
        (
            jnp.int32(0),
            crossed,
            unwritten((groups, TILE, cross_span), contrib.dtype),
            [unwritten((room, TILE, cross_span), contrib.dtype) for _, room in kinds],
        ),
    )

    my_far = held(plan["far"])
    my_far_round = held(plan["far_round"])

    def far_exchange(state):
        turn, buffer = state
        step = count(far_rounds <= turn)
        turn_of = turn - jnp.where(step > 0, far_rounds[jnp.maximum(step - 1, 0)], 0)
        chosen = my_far & (my_far_round == turn_of) & (my_group == (me ^ step))
        index = jnp.sum(chosen.astype(jnp.int32) * jnp.arange(groups))
        row = jnp.concatenate(
            [
                lax.dynamic_slice_in_dim(part, index, 1, 0)
                for part in recv + [cross_recv]
            ],
            axis=2,
        )
        arrived = lax.switch(
            step - 1,
            [lambda row, step=step: across(row, step) for step in range(1, groups)],
            row,
        )
        coming = (
            plan["far"]
            & for_me
            & (plan["far_round"] == turn_of)
            & (jnp.arange(groups)[None, :] == (me ^ step))
        )
        place = jnp.where(
            jnp.any(coming), jnp.sum(jnp.where(coming, plan["far_place"], 0)), groups
        )
        return (turn + 1, lax.dynamic_update_slice_in_dim(buffer, arrived, place, 0))

    far = unwritten((groups + 1, TILE, col_span + cross_span), contrib.dtype)
    _, far = lax.while_loop(
        lambda state: state[0] < far_rounds[-1], far_exchange, (jnp.int32(0), far)
    )

    schur, partial = assemble(
        row_code,
        row_from,
        starts,
        col_code,
        cross_rounds > 0,
        recv,
        near,
        far,
        cross_recv,
        cross_near,
        schur_init,
        block,
    )
    if n_col == 2:
        part = partial.shape[0] // n_col
        keep = lax.dynamic_slice_in_dim(partial, col_index * part, part, 0)
        give = lax.dynamic_slice_in_dim(partial, (1 - col_index) * part, part, 0)
        product = keep + lax.ppermute(give, "col", [(0, 1), (1, 0)])
    else:
        product = lax.psum_scatter(partial, "col", scatter_dimension=0, tiled=True)
    return (schur, product)


def takes_hops(n_row, n_col):
    return n_row == 4 and n_col == 2


def solution(mesh):
    in_specs = (
        P("front", None, None),
        P("front", "row", None),
        P("front", "row", "col"),
        P("front", None, None, None),
        P(),
        P(),
        P(),
        P(("front", "row"), "col"),
        P("col", None),
    )
    out_specs = (P(("front", "row"), "col"), P(("front", "row", "col"), None))

    return jax.shard_map(shards, mesh=mesh, in_specs=in_specs, out_specs=out_specs, check_vma=False)
```
